256 devices in a mesh: branch: 2 (over x_lo), strip: 128 (over y, z, x_hi, core).
Axes of the slice: x: 4 (x_hi: 2, x_lo: 2; x = x_hi * 2 + x_lo), y: 4, z: 8, core: 2. Of those that a mesh axis runs over, the one named last changes fastest.
Arguments:
- image_feats: bfloat16 [32, 16384, 256], P(None, ('branch', 'strip')), may hold values from -6 to 6
- cam_weights: bfloat16 [3, 9, 256, 256], replicated, may hold values from -0.1875 to 0.1875
- depth_weight: bfloat16 [256, 118], replicated, may hold values from -1.5 to 1.5
- ray_bins: int32 [16384, 118], P(('branch', 'strip')), may hold values from 0 to 16383, as said below
- pillar_sums: bfloat16 [32, 2048, 128], P(None, ('branch', 'strip')), may hold values from -12 to 12
- pillar_counts: int32 [32, 2048], P(None, ('branch', 'strip')), may hold values from 0 to 8
- lidar_weight: bfloat16 [4, 128, 128], replicated, may hold values from -0.375 to 0.375
- merge_weight: bfloat16 [9, 384, 256], replicated, may hold values from -0.15625 to 0.15625
- out_cotangent: bfloat16 [16, 1024, 256], P(None, ('branch', 'strip')), may hold values from -6 to 6
Outputs:
- merged: bfloat16 [16, 1024, 256], P(None, ('branch', 'strip'))
- cam_grad: bfloat16 [32, 16384, 256], P(None, ('branch', 'strip'))
- lid_grad: bfloat16 [16, 1024, 128], P(None, ('branch', 'strip'))
The draws below stay inside these ranges and needn't reach their ends.
Inputs may be any that keep to these rules, and one draw needn't show every extreme that they name: For a column j of sector s = j // 64, ray_bins[j, k] lies in sector s - 1, s or s + 1 taken modulo 256, in cycle k * 16 // 118.
All inputs are finite; a program needn't handle non-finite values.
Results may differ from the reference program's by a relative error of at most 0.014.
Values may be sent and summed in bfloat16 or wider, within the bound.
No kernel may reach another device: no remote copies, remote signals or barrier semaphores. Data moves between devices by JAX's collectives and lax.ppermute only.
A program may use at most 128 MiB of HBM per device.

```python
import jax
import jax.numpy as jnp
from jax import lax

C = 256
CL = 128
CF = 256
DB = 118
ROWS = 32
LAYERS = 3
COLS_DEV = 64
BR = 16
BA = 4
NSECT = 256
NCOL = 16384
NA = 1024
BCELL = 64
CC = 384


def draw_ray_bins(key, part):
    first_key, second_key = jax.random.split(jax.random.fold_in(key, 17))
    col_sector = (jnp.arange(NCOL, dtype=jnp.int32) // COLS_DEV)[:, None]
    steps = jax.random.randint(first_key, (NCOL, DB), -1, 2).astype(jnp.int32)
    slots = jax.random.randint(second_key, (NCOL, DB), 0, BA).astype(jnp.int32)
    cycles = (jnp.arange(DB, dtype=jnp.int32) * BR // DB)[None, :]
    sectors = (col_sector + steps) % NSECT
    return (sectors * (BR * BA) + cycles * BA + slots).astype(jnp.int32)


def plant(values, key, low, high):
    place = [jax.random.randint(jax.random.fold_in(key, axis), (), 0, length) for axis, length in enumerate(values.shape)]
    main_axis = values.shape.index(max(values.shape))
    neighbour = place[:main_axis] + [(place[main_axis] + 1) % values.shape[main_axis]] + place[main_axis + 1:]
    return values.at[tuple(place)].set(low).at[tuple(neighbour)].set(high)


def levels(stream_key, shape, cuts, smallest, largest):
    factor_of, own = 1.0, jax.random.fold_in(stream_key, 6)
    for axis_at, blocks in cuts:
        draws = jnp.exp(jax.random.uniform(jax.random.fold_in(own, axis_at), (blocks,), jnp.float32, smallest / len(cuts), largest / len(cuts)))
        factor_of = factor_of * jnp.repeat(draws, shape[axis_at] // blocks).reshape([-1 if axis == axis_at else 1 for axis in range(len(shape))])
    return factor_of


def gaussian(own_key, shape, scale, reach, pieces=(), held_as=jnp.bfloat16):
    array = scale * jax.random.normal(own_key, shape, jnp.float32)
    if pieces:
        array = array * levels(own_key, shape, pieces, -0.22, 0.18)
    return jnp.clip(array, -reach, reach).astype(held_as)


def setup_inputs(seed: int = 0) -> dict:
    key_of = jax.random.split(jax.random.key(seed), 10)
    return {
        "image_feats": gaussian(key_of[0], (ROWS, NCOL, C), 1.0, 6.0, ((1, 256),)),
        "cam_weights": gaussian(key_of[1], (LAYERS, 9, C, C), (9 * C // 2) ** -0.5, 0.1875),
        "depth_weight": gaussian(key_of[2], (C, DB), (C // 16) ** -0.5, 1.5),
        "ray_bins": draw_ray_bins(jax.random.fold_in(key_of[9], 71), 0),
        "pillar_sums": gaussian(key_of[4], (2 * BR, 2 * NA, CL), 2.0, 12.0, ((1, 256),)),
        "pillar_counts": plant(jax.random.randint(key_of[5], (2 * BR, 2 * NA), 0, 9), jax.random.fold_in(key_of[5], 1), 0, 8).astype(jnp.int32),
        "lidar_weight": gaussian(key_of[6], (4, CL, CL), (2 * CL) ** -0.5, 0.375),
        "merge_weight": gaussian(key_of[7], (9, CC, CF), (9 * CC // 2) ** -0.5, 0.15625),
        "out_cotangent": gaussian(key_of[8], (BR, NA, CF), 1.0, 6.0, ((1, 256),)),
    }


def wrap_columns(values):
    return jnp.concatenate([values[:, -1:], values, values[:, :1]], axis=1)


def pad_rows(values):
    return jnp.pad(values, ((1, 1), (0, 0), (0, 0)))


def conv_taps(padded, weights, row_count, col_count):
    result = None
    for tap_index in range(9):
        down_step = tap_index // 3
        right_step = tap_index % 3
        window = padded[down_step:down_step + row_count, right_step:right_step + col_count]
        partial_value = jnp.dot(window.reshape(row_count * col_count, -1), weights[tap_index], preferred_element_type=jnp.float32)
        result = partial_value if result is None else result + partial_value
    return result.reshape(row_count, col_count, -1)


def conv_back(padded, weights, row_count, col_count):
    result = None
    for tap_index in range(9):
        down_step = tap_index // 3
        right_step = tap_index % 3
        window = padded[2 - down_step:2 - down_step + row_count, 2 - right_step:2 - right_step + col_count]
        partial_value = lax.dot_general(window.reshape(row_count * col_count, -1), weights[tap_index], (((1,), (1,)), ((), ())), preferred_element_type=jnp.float32)
        result = partial_value if result is None else result + partial_value
    return result.reshape(row_count, col_count, -1)


def depth_part(block, depth_weight):
    logits = jnp.einsum("hjc,ck->hjk", block.astype(jnp.float32), depth_weight.astype(jnp.float32))
    softened = jax.nn.softplus(logits) + 0.05
    totals = jnp.sum(softened, axis=2, keepdims=True)
    depth_probs = softened / totals
    probs_low = depth_probs.astype(jnp.bfloat16)
    return logits, totals, depth_probs, probs_low


def reference(image_feats, cam_weights, depth_weight, ray_bins, pillar_sums, pillar_counts, lidar_weight, merge_weight, out_cotangent):
    features = image_feats
    for layer_idx in range(LAYERS):
        conv_out = conv_taps(pad_rows(wrap_columns(features)), cam_weights[layer_idx], ROWS, NCOL)
        features = jax.nn.relu(conv_out).astype(jnp.bfloat16)

    def lift_block(grid, sector):
        begin_col = (sector * COLS_DEV).astype(jnp.int32)
        block = lax.dynamic_slice_in_dim(features, begin_col, COLS_DEV, 1)
        bins = lax.dynamic_slice_in_dim(ray_bins, begin_col, COLS_DEV, 0).reshape(-1)
        logits, totals, depth_probs, probs_low = depth_part(block, depth_weight)
        lifted = jnp.einsum("hjk,hjc->jkc", probs_low.astype(jnp.float32), block.astype(jnp.float32))
        grid = grid + jax.ops.segment_sum(lifted.reshape(-1, C), bins, num_segments=NSECT * BCELL)
        return grid, None

    grid, _ = lax.scan(lift_block, jnp.zeros((NSECT * BCELL, C), jnp.float32), jnp.arange(NSECT, dtype=jnp.int32))
    cam_bev = grid.reshape(NSECT, BR, BA, C).transpose(1, 0, 2, 3).reshape(BR, NA, C).astype(jnp.bfloat16)

    occupied = (pillar_counts > 0).astype(jnp.float32)
    divisor = jnp.maximum(pillar_counts, 1).astype(jnp.float32)
    pillar_feat = (pillar_sums.astype(jnp.float32) * (occupied / divisor)[:, :, None]).astype(jnp.bfloat16)
    grouped = pillar_feat.reshape(BR, 2, NA, 2, CL)
    lidar_sum = None
    for offset in range(4):
        window = grouped[:, offset // 2, :, offset % 2, :].reshape(BR * NA, CL)
        partial_value = jnp.dot(window, lidar_weight[offset], preferred_element_type=jnp.float32)
        lidar_sum = partial_value if lidar_sum is None else lidar_sum + partial_value
    lid_bev = jax.nn.relu(lidar_sum).reshape(BR, NA, CL).astype(jnp.bfloat16)

    merged_in = jnp.concatenate([cam_bev, lid_bev], axis=2)
    pre_act = conv_taps(pad_rows(wrap_columns(merged_in)), merge_weight, BR, NA)
    merged = jax.nn.silu(pre_act).astype(jnp.bfloat16)
    gating = jax.nn.sigmoid(pre_act)
    slopes = gating * (1.0 + pre_act * (1.0 - gating))
    grad_pre = (out_cotangent.astype(jnp.float32) * slopes).astype(jnp.bfloat16)
    grad_in = conv_back(pad_rows(wrap_columns(grad_pre)), merge_weight, BR, NA)
    lid_grad = grad_in[:, :, C:].astype(jnp.bfloat16)
    cam_bev_grad = grad_in[:, :, :C].astype(jnp.bfloat16)
    grad_table = cam_bev_grad.reshape(BR, NSECT, BA, C).transpose(1, 0, 2, 3).reshape(NSECT * BCELL, C)

    def back_block(sector):
        begin_col = (sector * COLS_DEV).astype(jnp.int32)
        block = lax.dynamic_slice_in_dim(features, begin_col, COLS_DEV, 1)
        bins = lax.dynamic_slice_in_dim(ray_bins, begin_col, COLS_DEV, 0).reshape(-1)
        logits, totals, depth_probs, probs_low = depth_part(block, depth_weight)
        grad_lift = jnp.take(grad_table, bins, axis=0).reshape(COLS_DEV, DB, C)
        grad_probs = jnp.einsum("jkc,hjc->hjk", grad_lift.astype(jnp.float32), block.astype(jnp.float32))
        grad_direct = jnp.einsum("hjk,jkc->hjc", probs_low.astype(jnp.float32), grad_lift.astype(jnp.float32))
        grad_soft = (grad_probs - jnp.sum(grad_probs * depth_probs, axis=2, keepdims=True)) / totals
        grad_logits = (grad_soft * jax.nn.sigmoid(logits)).astype(jnp.bfloat16)
        grad_depth = jnp.einsum("hjk,ck->hjc", grad_logits.astype(jnp.float32), depth_weight.astype(jnp.float32))
        return (grad_direct + grad_depth).astype(jnp.bfloat16)

    blocks = lax.map(back_block, jnp.arange(NSECT, dtype=jnp.int32))
    cam_grad = blocks.transpose(1, 0, 2, 3).reshape(ROWS, NCOL, C)
    return merged, cam_grad, lid_grad
```

```python
import jax
import jax.numpy as jnp
from jax import lax
from jax.experimental import pallas as pl
from jax.experimental.pallas import tpu as pltpu
from jax.sharding import PartitionSpec as P

AXES = ("branch", "strip")
ROWS = 32
COLS = 64
WIDE = 80
C = 256
CL = 128
BINS = 118
LANES = 128
LAYERS = 3
BR = 16
BA = 4
WIN = 16
REACH = 6
SLOTS = 12
BLOCK = 8
TILE_H = 4
TILE = TILE_H * COLS
F32 = jnp.float32
BF16 = jnp.bfloat16


def whole(memory_space=pltpu.VMEM):
    return pl.BlockSpec(memory_space=memory_space)


def iota(shape, dim):
    return lax.broadcasted_iota(jnp.int32, shape, dim)


def nt_dot(lhs, rhs):
    return lax.dot_general(lhs, rhs, (((1,), (1,)), ((), ())), preferred_element_type=F32)


def tn_dot(lhs, rhs):
    return lax.dot_general(lhs, rhs, (((0,), (0,)), ((), ())), preferred_element_type=F32)


def dot(lhs, rhs):
    return jnp.dot(lhs, rhs, preferred_element_type=F32)


def fill_spread(spread):
    bin_index = iota((LANES, WIN * BR), 0)
    column = iota((LANES, WIN * BR), 1)
    for slot in range(SLOTS):
        offset = (column - (slot + 2) * BR) * BINS
        hit = (offset <= bin_index * BR) & (bin_index * BR < offset + BINS)
        spread[slot * LANES : (slot + 1) * LANES, :] = hit.astype(F32).astype(BF16)


def front_kernel(
    me_ref, image, from_right, from_left, weights, depth, bins,
    feat_out, share_out, lifted_out, probs_out, gain_out, slot_out,
    first, second, depth_pad, spread, masks,
):
    first[0] = jnp.zeros((WIDE, C), BF16)
    first[ROWS + 1] = jnp.zeros((WIDE, C), BF16)
    second[0] = jnp.zeros((WIDE, C), BF16)
    second[ROWS + 1] = jnp.zeros((WIDE, C), BF16)
    first[1 : ROWS + 1, 0:COLS, :] = image[...]
    first[1 : ROWS + 1, COLS:WIDE, :] = jnp.concatenate(
        [from_right[...], from_left[...]], axis=1
    )
    depth_pad[...] = jnp.zeros((C, LANES), BF16)
    depth_pad[:, 0:BINS] = depth[...]
    fill_spread(spread)
    cells = bins[...]
    sector = cells // (BR * BA)
    step = sector - me_ref[0] + 1
    step = jnp.where(step < 0, step + 256, step)
    step = jnp.where(step > 255, step - 256, step)
    slot = step * BA + cells % BA
    slot_out[...] = jnp.full((COLS, LANES), -1, jnp.int32)
    slot_out[:, 0:BINS] = slot
    slot_map = slot_out[...]
    for index in range(SLOTS):
        masks[index] = (slot_map == index).astype(F32).astype(BF16)

    def layer(source, target, index):
        @pl.loop(0, ROWS // BLOCK)
        def _(block):
            top = block * BLOCK
            lhs = jnp.concatenate(
                [
                    source[pl.ds(top + down, BLOCK)].reshape(BLOCK * WIDE, C)
                    for down in range(3)
                ],
                axis=1,
            )
            out = None
            for right in range(3):
                kernel = jnp.concatenate(
                    [weights[index, 3 * down + right] for down in range(3)], axis=0
                )
                part = dot(lhs, kernel).reshape(BLOCK, WIDE, C)
                if right != 1:
                    part = pltpu.roll(part, (1 - right) % WIDE, 1)
                out = part if out is None else out + part
            target[pl.ds(top + 1, BLOCK)] = jnp.maximum(out, 0.0).astype(BF16)

    layer(first, second, 0)
    layer(second, first, 1)
    layer(first, second, 2)

    lifted_out[...] = jnp.zeros((WIN * BR, C), F32)
    lane_ok = iota((TILE, LANES), 1) < BINS

    @pl.loop(0, ROWS // TILE_H)
    def _(tile):
        top = tile * TILE_H
        block = second[pl.ds(top + 1, TILE_H), 0:COLS, :].reshape(TILE, C)
        feat_out[pl.ds(tile * TILE, TILE), :] = block
        logits = dot(block, depth_pad[...])
        decay = jnp.exp(-jnp.abs(logits))
        soft = jnp.maximum(logits, 0.0) + jnp.log(1.0 + decay) + 0.05
        soft = jnp.where(lane_ok, soft, 0.0)
        scale = 1.0 / jnp.sum(soft, axis=1, keepdims=True)
        probs = soft * scale
        gate = jnp.where(logits >= 0.0, 1.0, decay) / (1.0 + decay)
        probs_out[pl.ds(tile * TILE, TILE), :] = probs
        gain_out[pl.ds(tile * TILE, TILE), :] = gate * scale
        low = probs.astype(BF16).reshape(TILE_H, COLS, LANES)
        share = dot(
            jnp.concatenate(
                [
                    (low * masks[index][None]).reshape(TILE, LANES)
                    for index in range(SLOTS)
                ],
                axis=1,
            ),
            spread[...],
        ).astype(BF16)
        share_out[pl.ds(tile * TILE, TILE), :] = share
        lifted_out[...] += tn_dot(share, block)


def front(me, image, from_right, from_left, weights, depth, bins):
    total = ROWS * COLS
    return pl.pallas_call(
        front_kernel,
        out_shape=(
            jax.ShapeDtypeStruct((total, C), BF16),
            jax.ShapeDtypeStruct((total, WIN * BR), BF16),
            jax.ShapeDtypeStruct((WIN * BR, C), F32),
            jax.ShapeDtypeStruct((total, LANES), F32),
            jax.ShapeDtypeStruct((total, LANES), F32),
            jax.ShapeDtypeStruct((COLS, LANES), jnp.int32),
        ),
        in_specs=[whole(pltpu.SMEM)] + [whole()] * 6,
        out_specs=(whole(),) * 6,
        scratch_shapes=[
            pltpu.VMEM((ROWS + 2, WIDE, C), BF16),
            pltpu.VMEM((ROWS + 2, WIDE, C), BF16),
            pltpu.VMEM((C, LANES), BF16),
            pltpu.VMEM((SLOTS * LANES, WIN * BR), BF16),
            pltpu.VMEM((SLOTS, COLS, LANES), BF16),
        ],
        compiler_params=pltpu.CompilerParams(vmem_limit_bytes=48 * 2**20),
        name="front",
    )(me, image, from_right, from_left, weights, depth, bins)


def along_cycles(part, down):
    if down == 0:
        return part
    cycle = iota(part.shape, 1)
    moved = pltpu.roll(part, down % BR, 1)
    keep = cycle >= 1 if down == 1 else cycle < BR - 1
    return jnp.where(keep, moved, 0.0)


def back_kernel(
    cam_window, lid_window, cot_window, weights, feat, share, probs, gain, slots, depth,
    merged_out, cam_out, lid_out,
    table, spread, wide_table, depth_pad,
):
    depth_pad[...] = jnp.zeros((C, LANES), BF16)
    depth_pad[:, 0:BINS] = depth[...]
    fill_spread(spread)
    merged_in = jnp.concatenate([cam_window[...].astype(BF16), lid_window[...]], axis=2)
    span = WIN - 2
    joined = jnp.concatenate(
        [merged_in[right : right + span].reshape(span * BR, C + CL) for right in range(3)],
        axis=1,
    )
    pre = None
    for down in range(3):
        kernel = jnp.concatenate([weights[3 * down + right] for right in range(3)], axis=0)
        part = along_cycles(dot(joined, kernel).reshape(span, BR, C), 1 - down)
        pre = part if pre is None else pre + part
    gate = 1.0 / (1.0 + jnp.exp(-pre))
    merged = (pre * gate).astype(BF16)
    grad_pre = (cot_window[...].astype(F32) * (gate * (1.0 + pre * (1.0 - gate)))).astype(BF16)
    inner = span - 2
    total = None
    for down in range(3):
        part = None
        for right in range(3):
            piece = nt_dot(
                grad_pre[2 - right : 2 - right + inner].reshape(inner * BR, C),
                weights[3 * down + right],
            )
            part = piece if part is None else part + piece
        part = along_cycles(part.reshape(inner, BR, C + CL), down - 1)
        total = part if total is None else total + part
    table[...] = jnp.zeros((WIN * BR, C), BF16)
    table[2 * BR : (WIN - 2) * BR, :] = total[:, :, 0:C].astype(BF16).reshape(inner * BR, C)
    order = iota((BR * BA, BR * BA), 0)
    source = iota((BR * BA, BR * BA), 1)
    swap = ((order % BA) * BR + order // BA == source).astype(F32).astype(BF16)
    own = merged[REACH - 1 : REACH - 1 + BA].reshape(BA * BR, C)
    merged_out[...] = dot(swap, own).astype(BF16)
    own_lid = total[REACH - 2 : REACH - 2 + BA, :, C:].astype(BF16).reshape(BA * BR, CL)
    lid_out[...] = dot(swap, own_lid).astype(BF16)
    wide_table[...] = dot(spread[...], table[...]).astype(BF16)

    @pl.loop(0, ROWS // TILE_H)
    def _(tile):
        rows = pl.ds(tile * TILE, TILE)
        block = feat[rows, :]
        slot_map = slots[...]
        picked = jnp.zeros((TILE_H, COLS, LANES), F32)
        for pair in range(SLOTS // 2):
            both = nt_dot(block, wide_table[pair * 2 * LANES : (pair + 1) * 2 * LANES, :])
            for side in range(2):
                value = both[:, side * LANES : (side + 1) * LANES].reshape(
                    TILE_H, COLS, LANES
                )
                picked = jnp.where((slot_map == 2 * pair + side)[None], value, picked)
        picked = picked.reshape(TILE, LANES)
        mean = jnp.sum(picked * probs[rows, :], axis=1, keepdims=True)
        grad_logits = ((picked - mean) * gain[rows, :]).astype(BF16)
        out = dot(share[rows, :], table[...]) + nt_dot(grad_logits, depth_pad[...])
        cam_out[pl.ds(tile * TILE_H, TILE_H)] = out.astype(BF16).reshape(TILE_H, COLS, C)


def back(cam_window, lid_window, cot_window, weights, feat, share, probs, gain, slots, depth):
    return pl.pallas_call(
        back_kernel,
        out_shape=(
            jax.ShapeDtypeStruct((BR * BA, C), BF16),
            jax.ShapeDtypeStruct((ROWS, COLS, C), BF16),
            jax.ShapeDtypeStruct((BR * BA, CL), BF16),
        ),
        in_specs=[whole()] * 10,
        out_specs=(whole(),) * 3,
        scratch_shapes=[
            pltpu.VMEM((WIN * BR, C), BF16),
            pltpu.VMEM((SLOTS * LANES, WIN * BR), BF16),
            pltpu.VMEM((SLOTS * LANES, C), BF16),
            pltpu.VMEM((C, LANES), BF16),
        ],
        compiler_params=pltpu.CompilerParams(vmem_limit_bytes=48 * 2**20),
        name="back",
    )(cam_window, lid_window, cot_window, weights, feat, share, probs, gain, slots, depth)


def shifted(block, distance):
    count = lax.axis_size(AXES)
    return lax.ppermute(block, AXES, [((i - distance) % count, i) for i in range(count)])


def local(
    image_feats, cam_weights, depth_weight, ray_bins, pillar_sums, pillar_counts,
    lidar_weight, merge_weight, out_cotangent,
):
    me = lax.axis_index(AXES).reshape(1).astype(jnp.int32)
    from_right = shifted(image_feats[:, 0:8], -1)
    from_left = shifted(image_feats[:, COLS - 8 :], 1)

    occupied = (pillar_counts > 0).astype(F32)
    divisor = jnp.maximum(pillar_counts, 1).astype(F32)
    pillar_feat = (pillar_sums.astype(F32) * (occupied / divisor)[:, :, None]).astype(BF16)
    grouped = pillar_feat.reshape(BR, 2, BA, 2, CL).transpose(2, 0, 1, 3, 4)
    lid_own = jax.nn.relu(
        dot(grouped.reshape(BA * BR, 4 * CL), lidar_weight.reshape(4 * CL, CL))
    ).astype(BF16).reshape(BA, BR, CL)
    cot_own = out_cotangent.transpose(1, 0, 2)
    side = jnp.concatenate([cot_own, lid_own], axis=2)
    side_right = shifted(side, -1)
    side_left = shifted(side, 1)

    feat, share, lifted, probs, gain, slots = front(
        me, image_feats, from_right, from_left, cam_weights, depth_weight, ray_bins
    )
    lifted = lifted.reshape(WIN, BR, C)
    low = lifted.astype(BF16)
    near_right = shifted(low[2:12], -1)
    near_left = shifted(low[4:14], 1)
    far_right = jnp.concatenate(
        [low[2:8].reshape(6, BR, C), ], axis=0
    ).at[4:6].add(near_right[0:2])
    far_left = low[8:14].at[0:2].add(near_left[8:10])
    far_right = shifted(far_right, -2)
    far_left = shifted(far_left, 2)
    side_far_right = shifted(side[0:2], -2)
    side_far_left = shifted(side[2:4], 2)
    window = lifted
    zero = lambda n: jnp.zeros((n, BR, C), F32)
    window = window + jnp.concatenate([zero(6), near_right.astype(F32)], 0)
    window = window + jnp.concatenate([near_left.astype(F32), zero(6)], 0)
    window = window + jnp.concatenate([far_left.astype(F32), zero(4), far_right.astype(F32)], 0)
    side_window = jnp.concatenate([side_far_left, side_left, side, side_right, side_far_right], 0)
    cot_window = side_window[1:15, :, 0:C]
    lid_window = side_window[:, :, C:]
    merged, cam_grad, lid_grad = back(
        window, lid_window, cot_window, merge_weight, feat, share, probs, gain, slots,
        depth_weight,
    )
    return (
        merged.reshape(BR, BA, C),
        cam_grad,
        lid_grad.reshape(BR, BA, CL),
    )


def solution(mesh):
    columns = P(None, AXES, None)
    placed = (
        columns, P(), P(), P(AXES, None), columns, P(None, AXES), P(), P(), columns,
    )
    return jax.shard_map(
        local, mesh=mesh, in_specs=placed, out_specs=(columns,) * 3, check_vma=False
    )
```

```python
import jax
import jax.numpy as jnp
from jax import lax
from jax.experimental import pallas as pl
from jax.experimental.pallas import tpu as pltpu
from jax.sharding import PartitionSpec as P

AXES = ("branch", "strip")
ROWS = 32
COLS = 64
WIDE = 80
C = 256
CL = 128
BINS = 118
LANES = 128
LAYERS = 3
BR = 16
BA = 4
WIN = 16
REACH = 6
SLOTS = 12
BLOCK = 8
TILE_H = 4
TILE = TILE_H * COLS
FUSE = 2
SPREAD = 2
F32 = jnp.float32
BF16 = jnp.bfloat16


def whole(memory_space=pltpu.VMEM):
    return pl.BlockSpec(memory_space=memory_space)


def iota(shape, dim):
    return lax.broadcasted_iota(jnp.int32, shape, dim)


def nt_dot(lhs, rhs):
    return lax.dot_general(lhs, rhs, (((1,), (1,)), ((), ())), preferred_element_type=F32)


def tn_dot(lhs, rhs):
    return lax.dot_general(lhs, rhs, (((0,), (0,)), ((), ())), preferred_element_type=F32)


def dot(lhs, rhs):
    return jnp.dot(lhs, rhs, preferred_element_type=F32)


def fill_spread(spread):
    bin_index = iota((LANES, WIN * BR), 0)
    column = iota((LANES, WIN * BR), 1)
    for slot in range(SLOTS):
        offset = (column - (slot + 2) * BR) * BINS
        hit = (offset <= bin_index * BR) & (bin_index * BR < offset + BINS)
        spread[slot * LANES : (slot + 1) * LANES, :] = hit.astype(F32).astype(BF16)


def fill_side(side, pillars, counts, lidar, cotangent, flat):
    for cycle in range(BR):
        flat[BA * cycle : BA * (cycle + 1), :] = cotangent[cycle].astype(F32)
    order = iota((BA * BR, BR * BA), 0)
    source = iota((BA * BR, BR * BA), 1)
    swap = ((order % BR) * BA + order // BR == source).astype(F32).astype(BF16)
    side[0:BA] = dot(swap, flat[...].astype(BF16)).astype(BF16).reshape(BA, BR, C)
    cells = 4 * BR * BA
    row = iota((cells, 2 * BR), 0)
    pick = (row // (2 * BA) == iota((cells, 2 * BR), 1)).astype(F32).astype(BF16)
    spread = nt_dot(pick, counts[...].astype(F32).astype(BF16))
    here = iota((cells, 2 * BA), 0) % (2 * BA) == iota((cells, 2 * BA), 1)
    count = jnp.sum(jnp.where(here, spread, 0.0), axis=1, keepdims=True)
    scale = jnp.where(count > 0.0, 1.0, 0.0) / jnp.maximum(count, 1.0)
    feats = (pillars[...].astype(F32).reshape(cells, CL) * scale).astype(BF16)
    goal = iota((BA * BR, cells), 0)
    origin = iota((BA * BR, cells), 1)
    base = (goal % BR) * (4 * BA) + (goal // BR) * 2
    total = None
    for offset in range(4):
        step = (offset // 2) * 2 * BA + offset % 2
        chosen = dot((base + step == origin).astype(F32).astype(BF16), feats).astype(BF16)
        part = dot(chosen, lidar[offset])
        total = part if total is None else total + part
    lid = jnp.maximum(total, 0.0).astype(BF16)
    for pair in range(2):
        top = pair * 2 * BR
        side[BA + pair] = jnp.concatenate(
            [lid[top : top + BR], lid[top + BR : top + 2 * BR]], axis=1
        )


def front_kernel(
    me_ref, image, from_right, from_left, weights, depth, bins,
    pillars, counts, lidar, cotangent,
    feat_out, share_out, lifted_out, note_out, far_out, probs_out, gain_out, slot_out,
    first, second, held, depth_pad, spread, masks, flat, sems,
):
    image_copy = pltpu.make_async_copy(
        image, first.at[pl.ds(1, ROWS), pl.ds(0, COLS)], sems.at[LAYERS]
    )
    image_copy.start()
    weight_copies = [
        pltpu.make_async_copy(weights.at[index], held.at[index], sems.at[index])
        for index in range(LAYERS)
    ]
    for copy in weight_copies:
        copy.start()
    first[0] = jnp.zeros((WIDE, C), BF16)
    first[ROWS + 1] = jnp.zeros((WIDE, C), BF16)
    second[0] = jnp.zeros((WIDE, C), BF16)
    second[ROWS + 1] = jnp.zeros((WIDE, C), BF16)
    first[1 : ROWS + 1, COLS:WIDE, :] = jnp.concatenate(
        [from_right[...], from_left[...]], axis=1
    )
    depth_pad[BINS - 6 :, :] = jnp.zeros((LANES - BINS + 6, C), BF16)
    depth_pad[0:BINS, :] = depth[...]
    fill_spread(spread)
    fill_side(note_out.at[pl.ds(WIN, 6)], pillars, counts, lidar, cotangent, flat)
    cells = bins[...]
    sector = cells // (BR * BA)
    step = sector - me_ref[0] + 1
    step = jnp.where(step < 0, step + 256, step)
    step = jnp.where(step > 255, step - 256, step)
    slot = step * BA + cells % BA
    slot_out[...] = jnp.full((COLS, LANES), -1, jnp.int32)
    slot_out[:, 0:BINS] = slot
    slot_map = slot_out[...]
    for index in range(SLOTS):
        masks[index] = (slot_map == index).astype(F32).astype(BF16)

    def convolved(source, index, top, narrow):
        lhs = jnp.concatenate(
            [
                source[pl.ds(top + down, BLOCK)].reshape(BLOCK * WIDE, C)
                for down in range(3)
            ],
            axis=1,
        )
        out = None
        for right in (1, 0, 2):
            kernel = jnp.concatenate(
                [held[index, 3 * down + right] for down in range(3)], axis=0
            )
            if narrow and right == 1:
                part = dot(
                    lhs.reshape(BLOCK, WIDE, 3 * C)[:, 0:COLS].reshape(BLOCK * COLS, 3 * C),
                    kernel,
                ).reshape(BLOCK, COLS, C)
            else:
                part = dot(lhs, kernel).reshape(BLOCK, WIDE, C)
                if right != 1:
                    part = pltpu.roll(part, (1 - right) % WIDE, 1)
                if narrow:
                    part = part[:, 0:COLS]
            out = part if out is None else out + part
        return jnp.maximum(out, 0.0).astype(BF16)

    def layer(source, target, index):
        weight_copies[index].wait()

        @pl.loop(0, ROWS // BLOCK, unroll=True)
        def _(block):
            target[pl.ds(block * BLOCK + 1, BLOCK)] = convolved(
                source, index, block * BLOCK, False
            )

    image_copy.wait()
    layer(first, second, 0)
    layer(second, first, 1)
    weight_copies[2].wait()

    lifted_out[...] = jnp.zeros((WIN * BR, C), F32)
    lane_ok = iota((TILE, LANES), 1) < BINS

    def lift(block, tile):
        rows = pl.ds(pl.multiple_of(tile * TILE, TILE), TILE)
        feat_out[rows, :] = block
        logits = nt_dot(block, depth_pad[...])
        decay = jnp.exp(-jnp.abs(logits))
        tail = jnp.log(1.0 + decay)
        soft = jnp.maximum(logits, 0.0) + tail + 0.05
        soft = jnp.where(lane_ok, soft, 0.0)
        scale = 1.0 / jnp.sum(soft, axis=1, keepdims=True)
        probs = soft * scale
        gate = jnp.exp(jnp.minimum(logits, 0.0) - tail)
        probs_out[rows, :] = probs
        gain_out[rows, :] = gate * scale
        low = probs.astype(BF16).reshape(TILE_H, COLS, LANES)
        share = dot(
            jnp.concatenate(
                [
                    (low * masks[index][None]).reshape(TILE, LANES)
                    for index in range(SLOTS)
                ],
                axis=1,
            ),
            spread[...],
        ).astype(BF16)
        share_out[rows, :] = share
        lifted_out[...] += tn_dot(share, block)

    @pl.loop(0, ROWS // BLOCK, unroll=FUSE)
    def _(block):
        made = convolved(first, 2, block * BLOCK, True)
        for part in range(BLOCK // TILE_H):
            lift(
                made[part * TILE_H : (part + 1) * TILE_H].reshape(TILE, C),
                block * (BLOCK // TILE_H) + part,
            )

    note_out[0:WIN] = lifted_out[...].astype(BF16).reshape(WIN, BR, C)
    odd = lax.rem(me_ref[0], 2)

    @pl.when(odd == 1)
    def _():
        far_out[...] = note_out[12:14]

    @pl.when(odd == 0)
    def _():
        far_out[...] = note_out[2:4]


def front(me, image, from_right, from_left, weights, depth, bins, pillars, counts, lidar, cotangent):
    total = ROWS * COLS
    return pl.pallas_call(
        front_kernel,
        out_shape=(
            jax.ShapeDtypeStruct((total, C), BF16),
            jax.ShapeDtypeStruct((total, WIN * BR), BF16),
            jax.ShapeDtypeStruct((WIN * BR, C), F32),
            jax.ShapeDtypeStruct((WIN + 6, BR, C), BF16),
            jax.ShapeDtypeStruct((2, BR, C), BF16),
            jax.ShapeDtypeStruct((total, LANES), F32),
            jax.ShapeDtypeStruct((total, LANES), F32),
            jax.ShapeDtypeStruct((COLS, LANES), jnp.int32),
        ),
        in_specs=[
            whole(pltpu.SMEM), whole(pl.ANY), whole(), whole(), whole(pl.ANY),
            whole(), whole(), whole(), whole(), whole(), whole(),
        ],
        out_specs=(whole(),) * 8,
        scratch_shapes=[
            pltpu.VMEM((ROWS + 2, WIDE, C), BF16),
            pltpu.VMEM((ROWS + 2, WIDE, C), BF16),
            pltpu.VMEM((LAYERS, 9, C, C), BF16),
            pltpu.VMEM((LANES, C), BF16),
            pltpu.VMEM((SLOTS * LANES, WIN * BR), BF16),
            pltpu.VMEM((SLOTS, COLS, LANES), BF16),
            pltpu.VMEM((BR * BA, C), F32),
            pltpu.SemaphoreType.DMA((LAYERS + 1,)),
        ],
        compiler_params=pltpu.CompilerParams(vmem_limit_bytes=48 * 2**20),
        name="front",
    )(me, image, from_right, from_left, weights, depth, bins, pillars, counts, lidar, cotangent)


def along_cycles(part, down):
    if down == 0:
        return part
    cycle = iota(part.shape, 1)
    moved = pltpu.roll(part, down % BR, 1)
    keep = cycle >= 1 if down == 1 else cycle < BR - 1
    return jnp.where(keep, moved, 0.0)


def back_kernel(
    me_ref, lifted, note, partner, crossed, relayed, far, weights, feat, share, probs, gain,
    slots, depth,
    merged_out, cam_out, lid_out,
    cam, cot, lid, table, spread, wide_table, depth_pad,
):
    depth_pad[BINS - 6 :, :] = jnp.zeros((LANES - BINS + 6, C), BF16)
    depth_pad[0:BINS, :] = depth[...]
    fill_spread(spread)

    def put_lid(at, packed):
        lid[at] = packed[:, 0:CL]
        lid[at + 1] = packed[:, CL:]

    cam[...] = lifted[...].reshape(WIN, BR, C)
    cot[REACH : REACH + BA] = note[WIN : WIN + BA]
    put_lid(REACH, note[WIN + BA])
    put_lid(REACH + 2, note[WIN + BA + 1])
    cot[0] = jnp.zeros((BR, C), BF16)
    cot[WIN - 1] = jnp.zeros((BR, C), BF16)
    odd = lax.rem(me_ref[0], 2)

    def gather(low_side):
        near = 10 if low_side else 2
        other = 2 if low_side else 10
        cam[6:16] += (partner[2:12] if low_side else crossed[0:10]).astype(F32)
        cam[0:10] += (crossed[0:10] if low_side else partner[4:14]).astype(F32)
        start = 10 if low_side else 0
        cam[start : start + 6] += relayed[0:6].astype(F32)
        edge = 0 if low_side else 14
        cam[edge : edge + 2] += far[...].astype(F32)
        cot[near : near + 4] = partner[WIN : WIN + 4]
        cot[other : other + 4] = crossed[10:14]
        cot[1 if low_side else 14] = crossed[14]
        cot[14 if low_side else 1] = relayed[6]
        put_lid(near, partner[WIN + 4])
        put_lid(near + 2, partner[WIN + 5])
        put_lid(other, crossed[15])
        put_lid(other + 2, crossed[16])
        put_lid(0 if low_side else 14, crossed[17])
        put_lid(14 if low_side else 0, relayed[7])

    @pl.when(odd == 0)
    def _():
        gather(True)

    @pl.when(odd == 1)
    def _():
        gather(False)

    span = WIN - 2
    merged_in = jnp.concatenate([cam[...].astype(BF16), lid[...]], axis=2)
    joined = jnp.concatenate(
        [merged_in[right : right + span].reshape(span * BR, C + CL) for right in range(3)],
        axis=1,
    )
    pre = None
    for down in range(3):
        kernel = jnp.concatenate([weights[3 * down + right] for right in range(3)], axis=0)
        part = along_cycles(dot(joined, kernel).reshape(span, BR, C), 1 - down)
        pre = part if pre is None else pre + part
    gate = 1.0 / (1.0 + jnp.exp(-pre))
    merged = (pre * gate).astype(BF16)
    grad_pre = (
        cot[1 : WIN - 1].astype(F32) * (gate * (1.0 + pre * (1.0 - gate)))
    ).astype(BF16)
    inner = span - 2
    total = None
    for down in range(3):
        part = None
        for right in range(3):
            piece = nt_dot(
                grad_pre[2 - right : 2 - right + inner].reshape(inner * BR, C),
                weights[3 * down + right],
            )
            part = piece if part is None else part + piece
        part = along_cycles(part.reshape(inner, BR, C + CL), down - 1)
        total = part if total is None else total + part
    table[0 : 2 * BR, :] = jnp.zeros((2 * BR, C), BF16)
    table[(WIN - 2) * BR :, :] = jnp.zeros((2 * BR, C), BF16)
    table[2 * BR : (WIN - 2) * BR, :] = total[:, :, 0:C].astype(BF16).reshape(inner * BR, C)
    order = iota((BR * BA, BR * BA), 0)
    source = iota((BR * BA, BR * BA), 1)
    swap = ((order % BA) * BR + order // BA == source).astype(F32).astype(BF16)
    own = merged[REACH - 1 : REACH - 1 + BA].reshape(BA * BR, C)
    turned = dot(swap, own)
    for cycle in range(BR):
        merged_out[cycle] = turned[BA * cycle : BA * (cycle + 1)].astype(BF16)
    own_lid = total[REACH - 2 : REACH - 2 + BA, :, C:].astype(BF16).reshape(BA * BR, CL)
    lid_out[...] = dot(swap, own_lid).astype(BF16)
    wide_table[...] = dot(spread[...], table[...]).astype(BF16)

    @pl.loop(0, ROWS // TILE_H, unroll=SPREAD)
    def _(tile):
        rows = pl.ds(pl.multiple_of(tile * TILE, TILE), TILE)
        block = feat[rows, :]
        slot_map = slots[...]
        picked = jnp.zeros((TILE_H, COLS, LANES), F32)
        for pair in range(SLOTS // 2):
            both = nt_dot(block, wide_table[pair * 2 * LANES : (pair + 1) * 2 * LANES, :])
            for side in range(2):
                value = both[:, side * LANES : (side + 1) * LANES].reshape(
                    TILE_H, COLS, LANES
                )
                picked = jnp.where((slot_map == 2 * pair + side)[None], value, picked)
        picked = picked.reshape(TILE, LANES)
        mean = jnp.sum(picked * probs[rows, :], axis=1, keepdims=True)
        grad_logits = ((picked - mean) * gain[rows, :]).astype(BF16)
        out = dot(share[rows, :], table[...]) + dot(grad_logits, depth_pad[...])
        cam_out[pl.ds(tile * TILE_H, TILE_H)] = out.astype(BF16).reshape(TILE_H, COLS, C)


def back(*operands):
    return pl.pallas_call(
        back_kernel,
        out_shape=(
            jax.ShapeDtypeStruct((BR, BA, C), BF16),
            jax.ShapeDtypeStruct((ROWS, COLS, C), BF16),
            jax.ShapeDtypeStruct((BR * BA, CL), BF16),
        ),
        in_specs=[whole(pltpu.SMEM)] + [whole()] * 13,
        out_specs=(whole(),) * 3,
        scratch_shapes=[
            pltpu.VMEM((WIN, BR, C), F32),
            pltpu.VMEM((WIN, BR, C), BF16),
            pltpu.VMEM((WIN, BR, CL), BF16),
            pltpu.VMEM((WIN * BR, C), BF16),
            pltpu.VMEM((SLOTS * LANES, WIN * BR), BF16),
            pltpu.VMEM((SLOTS * LANES, C), BF16),
            pltpu.VMEM((LANES, C), BF16),
        ],
        compiler_params=pltpu.CompilerParams(vmem_limit_bytes=48 * 2**20),
        name="back",
    )(*operands)


def shifted(block, distance):
    count = lax.axis_size(AXES)
    return lax.ppermute(block, AXES, [((i - distance) % count, i) for i in range(count)])


def swapped(block, odd_step):
    count = lax.axis_size(AXES)
    route = [(i, (i + odd_step if i % 2 else i - odd_step) % count) for i in range(count)]
    return lax.ppermute(block, AXES, route)


def local(
    image_feats, cam_weights, depth_weight, ray_bins, pillar_sums, pillar_counts,
    lidar_weight, merge_weight, out_cotangent,
):
    me = lax.axis_index(AXES).astype(jnp.int32)
    odd = me % 2 == 1
    me = me.reshape(1)
    from_right = shifted(image_feats[:, 0:8], -1)
    from_left = shifted(image_feats[:, COLS - 8 :], 1)
    depth = depth_weight.T
    feat, share, lifted, note, far, probs, gain, slots = front(
        me, image_feats, from_right, from_left, cam_weights, depth, ray_bins,
        pillar_sums, pillar_counts.T, lidar_weight, out_cotangent,
    )
    partner = swapped(note, -1)
    far_got = swapped(far, 3)
    wide = lambda a: a.astype(F32)
    four = jnp.zeros((4, BR, C), F32)
    mine = lifted.reshape(WIN, BR, C)
    rise = mine[2:12] + jnp.concatenate([four, wide(partner[2:8])], 0)
    fall = mine[4:14] + jnp.concatenate([wide(partner[8:14]), four], 0)
    crossing = jnp.concatenate(
        [
            jnp.where(odd, fall, rise).astype(BF16),
            note[16:20],
            jnp.where(odd, partner[19:20], partner[16:17]),
            note[20:22],
            jnp.where(odd, partner[21:22], partner[20:21]),
        ],
        axis=0,
    )
    crossed = swapped(crossing, 1)
    relay = jnp.concatenate(
        [
            jnp.where(odd, crossed[0:6], crossed[4:10]),
            jnp.where(odd, crossed[10:11], crossed[13:14]),
            jnp.where(odd, crossed[15:16], crossed[16:17]),
        ],
        axis=0,
    )
    relayed = swapped(relay, -1)
    merged, cam_grad, lid_grad = back(
        me, lifted, note, partner, crossed, relayed, far_got, merge_weight, feat, share,
        probs, gain, slots, depth,
    )
    return merged, cam_grad, lid_grad.reshape(BR, BA, CL)


def solution(mesh):
    columns = P(None, AXES, None)
    placed = (
        columns, P(), P(), P(AXES, None), columns, P(None, AXES), P(), P(), columns,
    )
    return jax.shard_map(
        local, mesh=mesh, in_specs=placed, out_specs=(columns,) * 3, check_vma=False
    )
```

```python
import jax
import jax.numpy as jnp
from jax import lax
from jax.experimental import pallas as pl
from jax.experimental.pallas import tpu as pltpu
from jax.sharding import PartitionSpec as P

AXES = ("branch", "strip")
ROWS = 32
COLS = 64
WIDE = 72
HALO = (WIDE - COLS) // 2
C = 256
CL = 128
BINS = 118
LANES = 128
LAYERS = 3
BR = 16
BA = 4
WIN = 16
REACH = 6
SLOTS = 12
BLOCK = 16
TILE_H = 4
TILE = TILE_H * COLS
UNROLL = 4
TALL_H = 16
TALL = TALL_H * COLS
F32 = jnp.float32
BF16 = jnp.bfloat16


def whole(memory_space=pltpu.VMEM):
    return pl.BlockSpec(memory_space=memory_space)


def iota(shape, dim):
    return lax.broadcasted_iota(jnp.int32, shape, dim)


def nt_dot(lhs, rhs):
    return lax.dot_general(lhs, rhs, (((1,), (1,)), ((), ())), preferred_element_type=F32)


def tn_dot(lhs, rhs):
    return lax.dot_general(lhs, rhs, (((0,), (0,)), ((), ())), preferred_element_type=F32)


def dot(lhs, rhs):
    return jnp.dot(lhs, rhs, preferred_element_type=F32)


def fill_spread(spread):
    bin_index = iota((LANES, WIN * BR), 0)
    column = iota((LANES, WIN * BR), 1)
    for slot in range(SLOTS):
        offset = (column - (slot + 2) * BR) * BINS
        hit = (offset <= bin_index * BR) & (bin_index * BR < offset + BINS)
        spread[slot * LANES : (slot + 1) * LANES, :] = hit.astype(F32).astype(BF16)


def fill_side(side, pillars, counts, lidar, cotangent, flat):
    for cycle in range(BR):
        flat[BA * cycle : BA * (cycle + 1), :] = cotangent[cycle].astype(F32)
    order = iota((BA * BR, BR * BA), 0)
    source = iota((BA * BR, BR * BA), 1)
    swap = ((order % BR) * BA + order // BR == source).astype(F32).astype(BF16)
    side[0:BA] = dot(swap, flat[...].astype(BF16)).astype(BF16).reshape(BA, BR, C)
    cells = 4 * BR * BA
    row = iota((cells, 2 * BR), 0)
    pick = (row // (2 * BA) == iota((cells, 2 * BR), 1)).astype(F32).astype(BF16)
    spread = nt_dot(pick, counts[...].astype(F32).astype(BF16))
    here = iota((cells, 2 * BA), 0) % (2 * BA) == iota((cells, 2 * BA), 1)
    count = jnp.sum(jnp.where(here, spread, 0.0), axis=1, keepdims=True)
    scale = jnp.where(count > 0.0, 1.0, 0.0) / jnp.maximum(count, 1.0)
    feats = (pillars[...].astype(F32).reshape(cells, CL) * scale).astype(BF16)
    goal = iota((BA * BR, cells), 0)
    origin = iota((BA * BR, cells), 1)
    base = (goal % BR) * (4 * BA) + (goal // BR) * 2
    total = None
    for offset in range(4):
        step = (offset // 2) * 2 * BA + offset % 2
        chosen = dot((base + step == origin).astype(F32).astype(BF16), feats).astype(BF16)
        part = dot(chosen, lidar[offset])
        total = part if total is None else total + part
    lid = jnp.maximum(total, 0.0).astype(BF16)
    for pair in range(2):
        top = pair * 2 * BR
        side[BA + pair] = jnp.concatenate(
            [lid[top : top + BR], lid[top + BR : top + 2 * BR]], axis=1
        )


def prepare_kernel(
    me_ref, image, weights, merging, depth_hbm, bins_hbm, pillars_hbm, counts_hbm, lidar_hbm,
    cotangent_hbm,
    padded, held, merge_held, spread, depth_pad, masks, slot_out, side,
    depth, bins, pillars, counts, lidar, cotangent, flat, sems,
):
    copies = [
        pltpu.make_async_copy(source, target, sems.at[index])
        for index, (source, target) in enumerate(
            [
                (depth_hbm, depth),
                (bins_hbm, bins),
                (pillars_hbm, pillars),
                (counts_hbm, counts),
                (lidar_hbm, lidar),
                (cotangent_hbm, cotangent),
                (image, padded.at[pl.ds(1, ROWS), pl.ds(0, COLS)]),
                (weights, held),
                (merging, merge_held),
            ]
        )
    ]
    for copy in copies:
        copy.start()
    padded[0] = jnp.zeros((WIDE, C), BF16)
    padded[ROWS + 1] = jnp.zeros((WIDE, C), BF16)
    fill_spread(spread)
    for copy in copies[:6]:
        copy.wait()
    depth_pad[BINS - 6 :, :] = jnp.zeros((LANES - BINS + 6, C), BF16)
    depth_pad[0:BINS, :] = depth[...]
    fill_side(side, pillars, counts, lidar, cotangent, flat)
    cells = bins[...]
    sector = cells // (BR * BA)
    step = sector - me_ref[0] + 1
    step = jnp.where(step < 0, step + 256, step)
    step = jnp.where(step > 255, step - 256, step)
    slot_out[...] = jnp.full((COLS, LANES), -1, jnp.int32)
    slot_out[:, 0:BINS] = step * BA + cells % BA
    slot_map = slot_out[...]
    for index in range(SLOTS):
        masks[index] = (slot_map == index).astype(F32).astype(BF16)
    for copy in copies[6:]:
        copy.wait()


def prepare(*operands):
    return pl.pallas_call(
        prepare_kernel,
        out_shape=(
            jax.ShapeDtypeStruct((ROWS + 2, WIDE, C), BF16),
            jax.ShapeDtypeStruct((LAYERS, 9, C, C), BF16),
            jax.ShapeDtypeStruct((9, C + CL, C), BF16),
            jax.ShapeDtypeStruct((SLOTS * LANES, WIN * BR), BF16),
            jax.ShapeDtypeStruct((LANES, C), BF16),
            jax.ShapeDtypeStruct((SLOTS, COLS, LANES), BF16),
            jax.ShapeDtypeStruct((COLS, LANES), jnp.int32),
            jax.ShapeDtypeStruct((6, BR, C), BF16),
        ),
        in_specs=[whole(pltpu.SMEM)] + [whole(pltpu.HBM)] * 9,
        out_specs=(whole(),) * 8,
        scratch_shapes=[
            pltpu.VMEM((BINS, C), BF16),
            pltpu.VMEM((COLS, BINS), jnp.int32),
            pltpu.VMEM((2 * BR, 2 * BA, CL), BF16),
            pltpu.VMEM((2 * BA, 2 * BR), jnp.int32),
            pltpu.VMEM((4, CL, CL), BF16),
            pltpu.VMEM((BR, BA, C), BF16),
            pltpu.VMEM((BR * BA, C), F32),
            pltpu.SemaphoreType.DMA((9,)),
        ],
        compiler_params=pltpu.CompilerParams(vmem_limit_bytes=24 * 2**20),
        cost_estimate=pl.CostEstimate(flops=10**8, bytes_accessed=8 * 2**20, transcendentals=0),
        name="prepare",
    )(*operands)


def front_kernel(
    me_ref, padded_in, from_right, from_left, held, depth_pad, spread, masks, side,
    first, feat_out, share_out, lifted_out, note_out, far_out, probs_out, gain_out,
    second,
):
    second[0] = jnp.zeros((WIDE, C), BF16)
    second[ROWS + 1] = jnp.zeros((WIDE, C), BF16)
    first[1 : ROWS + 1, COLS:WIDE, :] = jnp.concatenate(
        [from_right[...].astype(F32), from_left[...].astype(F32)], axis=1
    ).astype(BF16)
    note_out[WIN : WIN + 6] = side[...]

    def convolved(source, index, top, narrow):
        lhs = jnp.concatenate(
            [
                source[pl.ds(top + down, BLOCK)].reshape(BLOCK * WIDE, C)
                for down in range(3)
            ],
            axis=1,
        )
        out = None
        for right in (1, 0, 2):
            kernel = jnp.concatenate(
                [held[index, 3 * down + right] for down in range(3)], axis=0
            )
            if narrow and right == 1:
                part = dot(
                    lhs.reshape(BLOCK, WIDE, 3 * C)[:, 0:COLS].reshape(BLOCK * COLS, 3 * C),
                    kernel,
                ).reshape(BLOCK, COLS, C)
            else:
                part = dot(lhs, kernel).reshape(BLOCK, WIDE, C)
                if right != 1:
                    part = pltpu.roll(part, (1 - right) % WIDE, 1)
                if narrow:
                    part = part[:, 0:COLS]
            out = part if out is None else out + part
        return jnp.maximum(out, 0.0).astype(BF16)

    for index, (source, target) in enumerate([(first, second), (second, first)]):
        for block in range(ROWS // BLOCK):
            target[block * BLOCK + 1 : (block + 1) * BLOCK + 1] = convolved(
                source, index, block * BLOCK, False
            )
    for block in range(ROWS // BLOCK):
        feat_out[block * BLOCK * COLS : (block + 1) * BLOCK * COLS, :] = convolved(
            first, 2, block * BLOCK, True
        ).reshape(BLOCK * COLS, C)

    lane_ok = iota((TILE, LANES), 1) < BINS

    @pl.loop(0, ROWS // TILE_H, unroll=UNROLL)
    def _(tile):
        rows = pl.ds(pl.multiple_of(tile * TILE, TILE), TILE)
        logits = nt_dot(feat_out[rows, :], depth_pad[...])
        decay = jnp.exp(-jnp.abs(logits))
        tail = jnp.log(1.0 + decay)
        soft = jnp.maximum(logits, 0.0) + tail + 0.05
        soft = jnp.where(lane_ok, soft, 0.0)
        scale = 1.0 / jnp.sum(soft, axis=1, keepdims=True)
        probs = soft * scale
        gate = jnp.exp(jnp.minimum(logits, 0.0) - tail)
        probs_out[rows, :] = probs
        gain_out[rows, :] = gate * scale
        low = probs.astype(BF16).reshape(TILE_H, COLS, LANES)
        share_out[rows, :] = dot(
            jnp.concatenate(
                [
                    (low * masks[index][None]).reshape(TILE, LANES)
                    for index in range(SLOTS)
                ],
                axis=1,
            ),
            spread[...],
        ).astype(BF16)

    lifted = tn_dot(share_out[...], feat_out[...])
    lifted_out[...] = lifted
    note_out[0:WIN] = lifted.astype(BF16).reshape(WIN, BR, C)
    odd = lax.rem(me_ref[0], 2)

    @pl.when(odd == 1)
    def _():
        far_out[...] = note_out[12:14]

    @pl.when(odd == 0)
    def _():
        far_out[...] = note_out[2:4]


def front(*operands):
    total = ROWS * COLS
    return pl.pallas_call(
        front_kernel,
        out_shape=(
            jax.ShapeDtypeStruct((ROWS + 2, WIDE, C), BF16),
            jax.ShapeDtypeStruct((total, C), BF16),
            jax.ShapeDtypeStruct((total, WIN * BR), BF16),
            jax.ShapeDtypeStruct((WIN * BR, C), F32),
            jax.ShapeDtypeStruct((WIN + 6, BR, C), BF16),
            jax.ShapeDtypeStruct((2, BR, C), BF16),
            jax.ShapeDtypeStruct((total, LANES), F32),
            jax.ShapeDtypeStruct((total, LANES), F32),
        ),
        in_specs=[whole(pltpu.SMEM)] + [whole()] * 8,
        out_specs=(whole(),) * 8,
        scratch_shapes=[pltpu.VMEM((ROWS + 2, WIDE, C), BF16)],
        input_output_aliases={1: 0},
        compiler_params=pltpu.CompilerParams(vmem_limit_bytes=32 * 2**20),
        name="front",
    )(*operands)


def along_cycles(part, down):
    if down == 0:
        return part
    cycle = iota(part.shape, 1)
    moved = pltpu.roll(part, down % BR, 1)
    keep = cycle >= 1 if down == 1 else cycle < BR - 1
    return jnp.where(keep, moved, 0.0)


def back_kernel(
    me_ref, lifted, note, partner, crossed, relayed, far, weights, feat, share, probs, gain,
    slots, depth_pad, spread,
    merged_out, cam_out, lid_out,
    cam, cot, lid, table, wide_table,
):

    def put_lid(at, packed):
        lid[at] = packed[:, 0:CL]
        lid[at + 1] = packed[:, CL:]

    cam[...] = lifted[...].reshape(WIN, BR, C)
    cot[REACH : REACH + BA] = note[WIN : WIN + BA]
    put_lid(REACH, note[WIN + BA])
    put_lid(REACH + 2, note[WIN + BA + 1])
    cot[0] = jnp.zeros((BR, C), BF16)
    cot[WIN - 1] = jnp.zeros((BR, C), BF16)
    odd = lax.rem(me_ref[0], 2)

    def gather(low_side):
        near = 10 if low_side else 2
        other = 2 if low_side else 10
        cam[6:16] += (partner[2:12] if low_side else crossed[0:10]).astype(F32)
        cam[0:10] += (crossed[0:10] if low_side else partner[4:14]).astype(F32)
        start = 10 if low_side else 0
        cam[start : start + 6] += relayed[0:6].astype(F32)
        edge = 0 if low_side else 14
        cam[edge : edge + 2] += far[...].astype(F32)
        cot[near : near + 4] = partner[WIN : WIN + 4]
        cot[other : other + 4] = crossed[10:14]
        cot[1 if low_side else 14] = crossed[14]
        cot[14 if low_side else 1] = relayed[6]
        put_lid(near, partner[WIN + 4])
        put_lid(near + 2, partner[WIN + 5])
        put_lid(other, crossed[15])
        put_lid(other + 2, crossed[16])
        put_lid(0 if low_side else 14, crossed[17])
        put_lid(14 if low_side else 0, relayed[7])

    @pl.when(odd == 0)
    def _():
        gather(True)

    @pl.when(odd == 1)
    def _():
        gather(False)

    span = WIN - 2
    merged_in = jnp.concatenate([cam[...].astype(BF16), lid[...]], axis=2)
    joined = jnp.concatenate(
        [merged_in[right : right + span].reshape(span * BR, C + CL) for right in range(3)],
        axis=1,
    )
    pre = None
    for down in range(3):
        kernel = jnp.concatenate([weights[3 * down + right] for right in range(3)], axis=0)
        part = along_cycles(dot(joined, kernel).reshape(span, BR, C), 1 - down)
        pre = part if pre is None else pre + part
    gate = 1.0 / (1.0 + jnp.exp(-pre))
    merged = (pre * gate).astype(BF16)
    grad_pre = (
        cot[1 : WIN - 1].astype(F32) * (gate * (1.0 + pre * (1.0 - gate)))
    ).astype(BF16)
    inner = span - 2
    total = None
    for down in range(3):
        part = None
        for right in range(3):
            piece = nt_dot(
                grad_pre[2 - right : 2 - right + inner].reshape(inner * BR, C),
                weights[3 * down + right],
            )
            part = piece if part is None else part + piece
        part = along_cycles(part.reshape(inner, BR, C + CL), down - 1)
        total = part if total is None else total + part
    table[0 : 2 * BR, :] = jnp.zeros((2 * BR, C), BF16)
    table[(WIN - 2) * BR :, :] = jnp.zeros((2 * BR, C), BF16)
    table[2 * BR : (WIN - 2) * BR, :] = total[:, :, 0:C].astype(BF16).reshape(inner * BR, C)
    order = iota((BR * BA, BR * BA), 0)
    source = iota((BR * BA, BR * BA), 1)
    swap = ((order % BA) * BR + order // BA == source).astype(F32).astype(BF16)
    own = merged[REACH - 1 : REACH - 1 + BA].reshape(BA * BR, C)
    turned = dot(swap, own)
    for cycle in range(BR):
        merged_out[cycle] = turned[BA * cycle : BA * (cycle + 1)].astype(BF16)
    own_lid = total[REACH - 2 : REACH - 2 + BA, :, C:].astype(BF16).reshape(BA * BR, CL)
    lid_out[...] = dot(swap, own_lid).astype(BF16)
    wide_table[...] = dot(spread[...], table[...]).astype(BF16)

    @pl.loop(0, ROWS // TALL_H, unroll=True)
    def _(tile):
        rows = pl.ds(pl.multiple_of(tile * TALL, TALL), TALL)
        block = feat[rows, :]
        slot_map = slots[...]
        picked = jnp.zeros((TALL_H, COLS, LANES), F32)
        for pair in range(SLOTS // 2):
            both = nt_dot(block, wide_table[pair * 2 * LANES : (pair + 1) * 2 * LANES, :])
            for side in range(2):
                value = both[:, side * LANES : (side + 1) * LANES].reshape(
                    TALL_H, COLS, LANES
                )
                picked = jnp.where((slot_map == 2 * pair + side)[None], value, picked)
        picked = picked.reshape(TALL, LANES)
        mean = jnp.sum(picked * probs[rows, :], axis=1, keepdims=True)
        grad_logits = ((picked - mean) * gain[rows, :]).astype(BF16)
        out = dot(share[rows, :], table[...]) + dot(grad_logits, depth_pad[...])
        cam_out[pl.ds(tile * TALL_H, TALL_H)] = out.astype(BF16).reshape(TALL_H, COLS, C)


def back(*operands):
    return pl.pallas_call(
        back_kernel,
        out_shape=(
            jax.ShapeDtypeStruct((BR, BA, C), BF16),
            jax.ShapeDtypeStruct((ROWS, COLS, C), BF16),
            jax.ShapeDtypeStruct((BR * BA, CL), BF16),
        ),
        in_specs=[whole(pltpu.SMEM)] + [whole()] * 14,
        out_specs=(whole(),) * 3,
        scratch_shapes=[
            pltpu.VMEM((WIN, BR, C), F32),
            pltpu.VMEM((WIN, BR, C), BF16),
            pltpu.VMEM((WIN, BR, CL), BF16),
            pltpu.VMEM((WIN * BR, C), BF16),
            pltpu.VMEM((SLOTS * LANES, C), BF16),
        ],
        compiler_params=pltpu.CompilerParams(vmem_limit_bytes=32 * 2**20),
        name="back",
    )(*operands)


def shifted(block, distance):
    count = lax.axis_size(AXES)
    return lax.ppermute(block, AXES, [((i - distance) % count, i) for i in range(count)])


def swapped(block, odd_step):
    count = lax.axis_size(AXES)
    route = [(i, (i + odd_step if i % 2 else i - odd_step) % count) for i in range(count)]
    return lax.ppermute(block, AXES, route)


def local(
    image_feats, cam_weights, depth_weight, ray_bins, pillar_sums, pillar_counts,
    lidar_weight, merge_weight, out_cotangent,
):
    me = lax.axis_index(AXES).astype(jnp.int32)
    odd = me % 2 == 1
    me = me.reshape(1)
    from_right = shifted(image_feats[:, 0:HALO], -1)
    from_left = shifted(image_feats[:, COLS - HALO :], 1)
    padded, held, merge_held, spread, depth_pad, masks, slots, side = prepare(
        me,
        *[
            pltpu.with_memory_space_constraint(value, pltpu.HBM)
            for value in (
                image_feats, cam_weights, merge_weight, depth_weight.T, ray_bins, pillar_sums,
                pillar_counts.T, lidar_weight, out_cotangent,
            )
        ],
    )
    _, feat, share, lifted, note, far, probs, gain = front(
        me, padded, from_right, from_left, held, depth_pad, spread, masks, side
    )
    partner = swapped(note, -1)
    far_got = swapped(far, 3)
    wide = lambda a: a.astype(F32)
    four = jnp.zeros((4, BR, C), F32)
    mine = lifted.reshape(WIN, BR, C)
    rise = mine[2:12] + jnp.concatenate([four, wide(partner[2:8])], 0)
    fall = mine[4:14] + jnp.concatenate([wide(partner[8:14]), four], 0)
    crossing = jnp.concatenate(
        [
            jnp.where(odd, fall, rise).astype(BF16),
            note[16:20],
            jnp.where(odd, partner[19:20], partner[16:17]),
            note[20:22],
            jnp.where(odd, partner[21:22], partner[20:21]),
        ],
        axis=0,
    )
    crossed = swapped(crossing, 1)
    relay = jnp.concatenate(
        [
            jnp.where(odd, crossed[0:6], crossed[4:10]),
            jnp.where(odd, crossed[10:11], crossed[13:14]),
            jnp.where(odd, crossed[15:16], crossed[16:17]),
        ],
        axis=0,
    )
    relayed = swapped(relay, -1)
    merged, cam_grad, lid_grad = back(
        me, lifted, note, partner, crossed, relayed, far_got, merge_held, feat, share,
        probs, gain, slots, depth_pad, spread,
    )
    return merged, cam_grad, lid_grad.reshape(BR, BA, CL)


def solution(mesh):
    columns = P(None, AXES, None)
    placed = (
        columns, P(), P(), P(AXES, None), columns, P(None, AXES), P(), P(), columns,
    )
    return jax.shard_map(
        local, mesh=mesh, in_specs=placed, out_specs=(columns,) * 3, check_vma=False
    )
```

```python
import jax
import jax.numpy as jnp
from jax import lax
from jax.experimental import pallas as pl
from jax.experimental.pallas import tpu as pltpu
from jax.sharding import PartitionSpec as P

AXES = ("branch", "strip")
ROWS = 32
COLS = 64
WIDE = 72
HALO = (WIDE - COLS) // 2
C = 256
CL = 128
BINS = 118
LANES = 128
LAYERS = 3
BR = 16
BA = 4
WIN = 16
REACH = 6
SLOTS = 12
BLOCK = 16
TILE_H = 4
TILE = TILE_H * COLS
UNROLL = 4
TALL_H = 16
TALL = TALL_H * COLS
F32 = jnp.float32
BF16 = jnp.bfloat16


def whole(memory_space=pltpu.VMEM):
    return pl.BlockSpec(memory_space=memory_space)


def iota(shape, dim):
    return lax.broadcasted_iota(jnp.int32, shape, dim)


def nt_dot(lhs, rhs):
    return lax.dot_general(lhs, rhs, (((1,), (1,)), ((), ())), preferred_element_type=F32)


def tn_dot(lhs, rhs):
    return lax.dot_general(lhs, rhs, (((0,), (0,)), ((), ())), preferred_element_type=F32)


def dot(lhs, rhs):
    return jnp.dot(lhs, rhs, preferred_element_type=F32)


def fill_spread(spread):
    bin_index = iota((LANES, WIN * BR), 0)
    column = iota((LANES, WIN * BR), 1)
    for slot in range(SLOTS):
        offset = (column - (slot + 2) * BR) * BINS
        hit = (offset <= bin_index * BR) & (bin_index * BR < offset + BINS)
        spread[slot * LANES : (slot + 1) * LANES, :] = hit.astype(F32).astype(BF16)


def fill_side(side, pillars, counts, lidar, cotangent, flat):
    for cycle in range(BR):
        flat[BA * cycle : BA * (cycle + 1), :] = cotangent[cycle].astype(F32)
    order = iota((BA * BR, BR * BA), 0)
    source = iota((BA * BR, BR * BA), 1)
    swap = ((order % BR) * BA + order // BR == source).astype(F32).astype(BF16)
    side[0:BA] = dot(swap, flat[...].astype(BF16)).astype(BF16).reshape(BA, BR, C)
    cells = 4 * BR * BA
    row = iota((cells, 2 * BR), 0)
    pick = (row // (2 * BA) == iota((cells, 2 * BR), 1)).astype(F32).astype(BF16)
    spread = nt_dot(pick, counts[...].astype(F32).astype(BF16))
    here = iota((cells, 2 * BA), 0) % (2 * BA) == iota((cells, 2 * BA), 1)
    count = jnp.sum(jnp.where(here, spread, 0.0), axis=1, keepdims=True)
    scale = jnp.where(count > 0.0, 1.0, 0.0) / jnp.maximum(count, 1.0)
    feats = (pillars[...].astype(F32).reshape(cells, CL) * scale).astype(BF16)
    goal = iota((BA * BR, cells), 0)
    origin = iota((BA * BR, cells), 1)
    base = (goal % BR) * (4 * BA) + (goal // BR) * 2
    total = None
    for offset in range(4):
        step = (offset // 2) * 2 * BA + offset % 2
        chosen = dot((base + step == origin).astype(F32).astype(BF16), feats).astype(BF16)
        part = dot(chosen, lidar[offset])
        total = part if total is None else total + part
    lid = jnp.maximum(total, 0.0).astype(BF16)
    for pair in range(2):
        top = pair * 2 * BR
        side[BA + pair] = jnp.concatenate(
            [lid[top : top + BR], lid[top + BR : top + 2 * BR]], axis=1
        )


def prepare_kernel(
    me_ref, image, weights, depth_hbm, bins_hbm, pillars_hbm, counts_hbm, lidar_hbm,
    cotangent_hbm,
    padded, held, spread, depth_pad, masks, slot_out, side,
    depth, bins, pillars, counts, lidar, cotangent, flat, sems,
):
    copies = [
        pltpu.make_async_copy(source, target, sems.at[index])
        for index, (source, target) in enumerate(
            [
                (depth_hbm, depth),
                (bins_hbm, bins),
                (pillars_hbm, pillars),
                (counts_hbm, counts),
                (lidar_hbm, lidar),
                (cotangent_hbm, cotangent),
                (image, padded.at[pl.ds(1, ROWS), pl.ds(0, COLS)]),
                (weights.at[0], held),
            ]
        )
    ]
    for copy in copies:
        copy.start()
    padded[0] = jnp.zeros((WIDE, C), BF16)
    padded[ROWS + 1] = jnp.zeros((WIDE, C), BF16)
    fill_spread(spread)
    for copy in copies[:6]:
        copy.wait()
    depth_pad[BINS - 6 :, :] = jnp.zeros((LANES - BINS + 6, C), BF16)
    depth_pad[0:BINS, :] = depth[...]
    fill_side(side, pillars, counts, lidar, cotangent, flat)
    cells = bins[...]
    sector = cells // (BR * BA)
    step = sector - me_ref[0] + 1
    step = jnp.where(step < 0, step + 256, step)
    step = jnp.where(step > 255, step - 256, step)
    slot_out[...] = jnp.full((COLS, LANES), -1, jnp.int32)
    slot_out[:, 0:BINS] = step * BA + cells % BA
    slot_map = slot_out[...]
    for index in range(SLOTS):
        masks[index] = (slot_map == index).astype(F32).astype(BF16)
    for copy in copies[6:]:
        copy.wait()


def prepare(*operands):
    return pl.pallas_call(
        prepare_kernel,
        out_shape=(
            jax.ShapeDtypeStruct((ROWS + 2, WIDE, C), BF16),
            jax.ShapeDtypeStruct((9, C, C), BF16),
            jax.ShapeDtypeStruct((SLOTS * LANES, WIN * BR), BF16),
            jax.ShapeDtypeStruct((LANES, C), BF16),
            jax.ShapeDtypeStruct((SLOTS, COLS, LANES), BF16),
            jax.ShapeDtypeStruct((COLS, LANES), jnp.int32),
            jax.ShapeDtypeStruct((6, BR, C), BF16),
        ),
        in_specs=[whole(pltpu.SMEM)] + [whole(pltpu.HBM)] * 8,
        out_specs=(whole(),) * 7,
        scratch_shapes=[
            pltpu.VMEM((BINS, C), BF16),
            pltpu.VMEM((COLS, BINS), jnp.int32),
            pltpu.VMEM((2 * BR, 2 * BA, CL), BF16),
            pltpu.VMEM((2 * BA, 2 * BR), jnp.int32),
            pltpu.VMEM((4, CL, CL), BF16),
            pltpu.VMEM((BR, BA, C), BF16),
            pltpu.VMEM((BR * BA, C), F32),
            pltpu.SemaphoreType.DMA((8,)),
        ],
        compiler_params=pltpu.CompilerParams(vmem_limit_bytes=24 * 2**20),
        cost_estimate=pl.CostEstimate(flops=10**8, bytes_accessed=8 * 2**20, transcendentals=0),
        name="prepare",
    )(*operands)


def front_kernel(
    me_ref, padded_in, crossed, beside, held_first, depth_pad, spread, masks, side,
    weights, merging,
    first, feat_out, share_out, lifted_out, note_out, far_out, probs_out, gain_out, merge_held,
    second, held_rest, sems,
):
    copies = [
        pltpu.make_async_copy(weights.at[1], held_rest.at[0], sems.at[0]),
        pltpu.make_async_copy(weights.at[2], held_rest.at[1], sems.at[1]),
        pltpu.make_async_copy(merging, merge_held, sems.at[2]),
    ]
    for copy in copies:
        copy.start()
    odd = lax.rem(me_ref[0], 2)
    second[0] = jnp.zeros((WIDE, C), BF16)
    second[ROWS + 1] = jnp.zeros((WIDE, C), BF16)

    def put_halo(right, left):
        first[1 : ROWS + 1, COLS:WIDE, :] = jnp.concatenate(
            [right[...].astype(F32), left[...].astype(F32)], axis=1
        ).astype(BF16)

    @pl.when(odd == 1)
    def _():
        put_halo(crossed, beside)

    @pl.when(odd == 0)
    def _():
        put_halo(beside, crossed)

    note_out[WIN : WIN + 6] = side[...]

    def convolved(source, held, top, narrow):
        lhs = jnp.concatenate(
            [
                source[pl.ds(top + down, BLOCK)].reshape(BLOCK * WIDE, C)
                for down in range(3)
            ],
            axis=1,
        )
        out = None
        for right in (1, 0, 2):
            kernel = jnp.concatenate(
                [held[3 * down + right] for down in range(3)], axis=0
            )
            if narrow and right == 1:
                part = dot(
                    lhs.reshape(BLOCK, WIDE, 3 * C)[:, 0:COLS].reshape(BLOCK * COLS, 3 * C),
                    kernel,
                ).reshape(BLOCK, COLS, C)
            else:
                part = dot(lhs, kernel).reshape(BLOCK, WIDE, C)
                if right != 1:
                    part = pltpu.roll(part, (1 - right) % WIDE, 1)
                if narrow:
                    part = part[:, 0:COLS]
            out = part if out is None else out + part
        return jnp.maximum(out, 0.0).astype(BF16)

    for index, (source, target) in enumerate([(first, second), (second, first)]):
        if index == 1:
            copies[0].wait()
        held = held_first if index == 0 else held_rest.at[0]
        for block in range(ROWS // BLOCK):
            target[block * BLOCK + 1 : (block + 1) * BLOCK + 1] = convolved(
                source, held, block * BLOCK, False
            )
    copies[1].wait()
    for block in range(ROWS // BLOCK):
        feat_out[block * BLOCK * COLS : (block + 1) * BLOCK * COLS, :] = convolved(
            first, held_rest.at[1], block * BLOCK, True
        ).reshape(BLOCK * COLS, C)

    lane_ok = iota((TILE, LANES), 1) < BINS

    @pl.loop(0, ROWS // TILE_H, unroll=UNROLL)
    def _(tile):
        rows = pl.ds(pl.multiple_of(tile * TILE, TILE), TILE)
        logits = nt_dot(feat_out[rows, :], depth_pad[...])
        decay = jnp.exp(-jnp.abs(logits))
        tail = jnp.log(1.0 + decay)
        soft = jnp.maximum(logits, 0.0) + tail + 0.05
        soft = jnp.where(lane_ok, soft, 0.0)
        scale = 1.0 / jnp.sum(soft, axis=1, keepdims=True)
        probs = soft * scale
        gate = jnp.exp(jnp.minimum(logits, 0.0) - tail)
        probs_out[rows, :] = probs
        gain_out[rows, :] = gate * scale
        low = probs.astype(BF16).reshape(TILE_H, COLS, LANES)
        share_out[rows, :] = dot(
            jnp.concatenate(
                [
                    (low * masks[index][None]).reshape(TILE, LANES)
                    for index in range(SLOTS)
                ],
                axis=1,
            ),
            spread[...],
        ).astype(BF16)

    lifted = tn_dot(share_out[...], feat_out[...])
    lifted_out[...] = lifted
    note_out[0:WIN] = lifted.astype(BF16).reshape(WIN, BR, C)
    copies[2].wait()

    @pl.when(odd == 1)
    def _():
        far_out[...] = note_out[12:14]

    @pl.when(odd == 0)
    def _():
        far_out[...] = note_out[2:4]


def front(*operands):
    total = ROWS * COLS
    return pl.pallas_call(
        front_kernel,
        out_shape=(
            jax.ShapeDtypeStruct((ROWS + 2, WIDE, C), BF16),
            jax.ShapeDtypeStruct((total, C), BF16),
            jax.ShapeDtypeStruct((total, WIN * BR), BF16),
            jax.ShapeDtypeStruct((WIN * BR, C), F32),
            jax.ShapeDtypeStruct((WIN + 6, BR, C), BF16),
            jax.ShapeDtypeStruct((2, BR, C), BF16),
            jax.ShapeDtypeStruct((total, LANES), F32),
            jax.ShapeDtypeStruct((total, LANES), F32),
            jax.ShapeDtypeStruct((9, C + CL, C), BF16),
        ),
        in_specs=[whole(pltpu.SMEM)] + [whole()] * 8 + [whole(pltpu.HBM)] * 2,
        out_specs=(whole(),) * 9,
        scratch_shapes=[
            pltpu.VMEM((ROWS + 2, WIDE, C), BF16),
            pltpu.VMEM((LAYERS - 1, 9, C, C), BF16),
            pltpu.SemaphoreType.DMA((3,)),
        ],
        input_output_aliases={1: 0},
        compiler_params=pltpu.CompilerParams(vmem_limit_bytes=32 * 2**20),
        name="front",
    )(*operands)


def along_cycles(part, down):
    if down == 0:
        return part
    cycle = iota(part.shape, 1)
    moved = pltpu.roll(part, down % BR, 1)
    keep = cycle >= 1 if down == 1 else cycle < BR - 1
    return jnp.where(keep, moved, 0.0)


def back_kernel(
    me_ref, lifted, note, partner, crossed, relayed, far, weights, feat, share, probs, gain,
    slots, depth_pad, spread,
    merged_out, cam_out, lid_out,
    cam, cot, lid, table, wide_table,
):

    def put_lid(at, packed):
        lid[at] = packed[:, 0:CL]
        lid[at + 1] = packed[:, CL:]

    cam[...] = lifted[...].reshape(WIN, BR, C)
    cot[REACH : REACH + BA] = note[WIN : WIN + BA]
    put_lid(REACH, note[WIN + BA])
    put_lid(REACH + 2, note[WIN + BA + 1])
    cot[0] = jnp.zeros((BR, C), BF16)
    cot[WIN - 1] = jnp.zeros((BR, C), BF16)
    odd = lax.rem(me_ref[0], 2)

    def gather(low_side):
        near = 10 if low_side else 2
        other = 2 if low_side else 10
        cam[6:16] += (partner[2:12] if low_side else crossed[0:10]).astype(F32)
        cam[0:10] += (crossed[0:10] if low_side else partner[4:14]).astype(F32)
        start = 10 if low_side else 0
        cam[start : start + 6] += relayed[0:6].astype(F32)
        edge = 0 if low_side else 14
        cam[edge : edge + 2] += far[...].astype(F32)
        cot[near : near + 4] = partner[WIN : WIN + 4]
        cot[other : other + 4] = crossed[10:14]
        cot[1 if low_side else 14] = crossed[14]
        cot[14 if low_side else 1] = relayed[6]
        put_lid(near, partner[WIN + 4])
        put_lid(near + 2, partner[WIN + 5])
        put_lid(other, crossed[15])
        put_lid(other + 2, crossed[16])
        put_lid(0 if low_side else 14, crossed[17])
        put_lid(14 if low_side else 0, relayed[7])

    @pl.when(odd == 0)
    def _():
        gather(True)

    @pl.when(odd == 1)
    def _():
        gather(False)

    span = WIN - 2
    merged_in = jnp.concatenate([cam[...].astype(BF16), lid[...]], axis=2)
    joined = jnp.concatenate(
        [merged_in[right : right + span].reshape(span * BR, C + CL) for right in range(3)],
        axis=1,
    )
    pre = None
    for down in range(3):
        kernel = jnp.concatenate([weights[3 * down + right] for right in range(3)], axis=0)
        part = along_cycles(dot(joined, kernel).reshape(span, BR, C), 1 - down)
        pre = part if pre is None else pre + part
    gate = 1.0 / (1.0 + jnp.exp(-pre))
    merged = (pre * gate).astype(BF16)
    grad_pre = (
        cot[1 : WIN - 1].astype(F32) * (gate * (1.0 + pre * (1.0 - gate)))
    ).astype(BF16)
    inner = span - 2
    total = None
    for down in range(3):
        part = None
        for right in range(3):
            piece = nt_dot(
                grad_pre[2 - right : 2 - right + inner].reshape(inner * BR, C),
                weights[3 * down + right],
            )
            part = piece if part is None else part + piece
        part = along_cycles(part.reshape(inner, BR, C + CL), down - 1)
        total = part if total is None else total + part
    table[0 : 2 * BR, :] = jnp.zeros((2 * BR, C), BF16)
    table[(WIN - 2) * BR :, :] = jnp.zeros((2 * BR, C), BF16)
    table[2 * BR : (WIN - 2) * BR, :] = total[:, :, 0:C].astype(BF16).reshape(inner * BR, C)
    order = iota((BR * BA, BR * BA), 0)
    source = iota((BR * BA, BR * BA), 1)
    swap = ((order % BA) * BR + order // BA == source).astype(F32).astype(BF16)
    own = merged[REACH - 1 : REACH - 1 + BA].reshape(BA * BR, C)
    turned = dot(swap, own)
    for cycle in range(BR):
        merged_out[cycle] = turned[BA * cycle : BA * (cycle + 1)].astype(BF16)
    own_lid = total[REACH - 2 : REACH - 2 + BA, :, C:].astype(BF16).reshape(BA * BR, CL)
    lid_out[...] = dot(swap, own_lid).astype(BF16)
    wide_table[...] = dot(spread[...], table[...]).astype(BF16)

    @pl.loop(0, ROWS // TALL_H, unroll=True)
    def _(tile):
        rows = pl.ds(pl.multiple_of(tile * TALL, TALL), TALL)
        block = feat[rows, :]
        slot_map = slots[...]
        picked = jnp.zeros((TALL_H, COLS, LANES), F32)
        for pair in range(SLOTS // 2):
            both = nt_dot(block, wide_table[pair * 2 * LANES : (pair + 1) * 2 * LANES, :])
            for side in range(2):
                value = both[:, side * LANES : (side + 1) * LANES].reshape(
                    TALL_H, COLS, LANES
                )
                picked = jnp.where((slot_map == 2 * pair + side)[None], value, picked)
        picked = picked.reshape(TALL, LANES)
        mean = jnp.sum(picked * probs[rows, :], axis=1, keepdims=True)
        grad_logits = ((picked - mean) * gain[rows, :]).astype(BF16)
        out = dot(share[rows, :], table[...]) + dot(grad_logits, depth_pad[...])
        cam_out[pl.ds(tile * TALL_H, TALL_H)] = out.astype(BF16).reshape(TALL_H, COLS, C)


def back(*operands):
    return pl.pallas_call(
        back_kernel,
        out_shape=(
            jax.ShapeDtypeStruct((BR, BA, C), BF16),
            jax.ShapeDtypeStruct((ROWS, COLS, C), BF16),
            jax.ShapeDtypeStruct((BR * BA, CL), BF16),
        ),
        in_specs=[whole(pltpu.SMEM)] + [whole()] * 14,
        out_specs=(whole(),) * 3,
        scratch_shapes=[
            pltpu.VMEM((WIN, BR, C), F32),
            pltpu.VMEM((WIN, BR, C), BF16),
            pltpu.VMEM((WIN, BR, CL), BF16),
            pltpu.VMEM((WIN * BR, C), BF16),
            pltpu.VMEM((SLOTS * LANES, C), BF16),
        ],
        compiler_params=pltpu.CompilerParams(vmem_limit_bytes=32 * 2**20),
        name="back",
    )(*operands)


def swapped(block, odd_step):
    count = lax.axis_size(AXES)
    route = [(i, (i + odd_step if i % 2 else i - odd_step) % count) for i in range(count)]
    return lax.ppermute(block, AXES, route)


def local(
    image_feats, cam_weights, depth_weight, ray_bins, pillar_sums, pillar_counts,
    lidar_weight, merge_weight, out_cotangent,
):
    me = lax.axis_index(AXES).astype(jnp.int32)
    odd = me % 2 == 1
    me = me.reshape(1)
    left_edge = image_feats[:, 0:HALO]
    right_edge = image_feats[:, COLS - HALO :]
    beside = swapped(jnp.where(odd, left_edge, right_edge), -1)
    across = swapped(jnp.where(odd, right_edge, left_edge), 1)
    pinned = lambda value: pltpu.with_memory_space_constraint(value, pltpu.HBM)
    padded, held, spread, depth_pad, masks, slots, side = prepare(
        me,
        *[
            pinned(value)
            for value in (
                image_feats, cam_weights, depth_weight.T, ray_bins, pillar_sums,
                pillar_counts.T, lidar_weight, out_cotangent,
            )
        ],
    )
    _, feat, share, lifted, note, far, probs, gain, merge_held = front(
        me, padded, across, beside, held, depth_pad, spread, masks, side,
        pinned(cam_weights), pinned(merge_weight),
    )
    partner = swapped(note, -1)
    far_got = swapped(far, 3)
    wide = lambda a: a.astype(F32)
    four = jnp.zeros((4, BR, C), F32)
    mine = lifted.reshape(WIN, BR, C)
    rise = mine[2:12] + jnp.concatenate([four, wide(partner[2:8])], 0)
    fall = mine[4:14] + jnp.concatenate([wide(partner[8:14]), four], 0)
    crossing = jnp.concatenate(
        [
            jnp.where(odd, fall, rise).astype(BF16),
            note[16:20],
            jnp.where(odd, partner[19:20], partner[16:17]),
            note[20:22],
            jnp.where(odd, partner[21:22], partner[20:21]),
        ],
        axis=0,
    )
    crossed = swapped(crossing, 1)
    relay = jnp.concatenate(
        [
            jnp.where(odd, crossed[0:6], crossed[4:10]),
            jnp.where(odd, crossed[10:11], crossed[13:14]),
            jnp.where(odd, crossed[15:16], crossed[16:17]),
        ],
        axis=0,
    )
    relayed = swapped(relay, -1)
    merged, cam_grad, lid_grad = back(
        me, lifted, note, partner, crossed, relayed, far_got, merge_held, feat, share,
        probs, gain, slots, depth_pad, spread,
    )
    return merged, cam_grad, lid_grad.reshape(BR, BA, CL)


def solution(mesh):
    columns = P(None, AXES, None)
    placed = (
        columns, P(), P(), P(AXES, None), columns, P(None, AXES), P(), P(), columns,
    )
    return jax.shard_map(
        local, mesh=mesh, in_specs=placed, out_specs=(columns,) * 3, check_vma=False
    )
```

```python
import jax
import jax.numpy as jnp
from jax import lax
from jax.experimental import pallas as pl
from jax.experimental.pallas import tpu as pltpu
from jax.sharding import PartitionSpec as P

AXES = ("branch", "strip")
ROWS = 32
COLS = 64
WIDE = 72
HALO = (WIDE - COLS) // 2
C = 256
CL = 128
BINS = 118
LANES = 128
LAYERS = 3
BR = 16
BA = 4
WIN = 16
REACH = 6
SLOTS = 12
BLOCK = 16
TILE_H = 4
TILE = TILE_H * COLS
UNROLL = 4
TALL_H = 16
TALL = TALL_H * COLS
F32 = jnp.float32
BF16 = jnp.bfloat16


def whole(memory_space=pltpu.VMEM):
    return pl.BlockSpec(memory_space=memory_space)


def iota(shape, dim):
    return lax.broadcasted_iota(jnp.int32, shape, dim)


def nt_dot(lhs, rhs):
    return lax.dot_general(lhs, rhs, (((1,), (1,)), ((), ())), preferred_element_type=F32)


def tn_dot(lhs, rhs):
    return lax.dot_general(lhs, rhs, (((0,), (0,)), ((), ())), preferred_element_type=F32)


def dot(lhs, rhs):
    return jnp.dot(lhs, rhs, preferred_element_type=F32)


def fill_spread(spread):
    bin_index = iota((LANES, WIN * BR), 0)
    column = iota((LANES, WIN * BR), 1)
    for slot in range(SLOTS):
        offset = (column - (slot + 2) * BR) * BINS
        hit = (offset <= bin_index * BR) & (bin_index * BR < offset + BINS)
        spread[slot * LANES : (slot + 1) * LANES, :] = hit.astype(F32).astype(BF16)


def fill_side(side, pillars, counts, lidar, cotangent, flat):
    for cycle in range(BR):
        flat[BA * cycle : BA * (cycle + 1), :] = cotangent[cycle].astype(F32)
    order = iota((BA * BR, BR * BA), 0)
    source = iota((BA * BR, BR * BA), 1)
    swap = ((order % BR) * BA + order // BR == source).astype(F32).astype(BF16)
    side[0:BA] = dot(swap, flat[...].astype(BF16)).astype(BF16).reshape(BA, BR, C)
    cells = 4 * BR * BA
    row = iota((cells, 2 * BR), 0)
    pick = (row // (2 * BA) == iota((cells, 2 * BR), 1)).astype(F32).astype(BF16)
    spread = nt_dot(pick, counts[...].astype(F32).astype(BF16))
    here = iota((cells, 2 * BA), 0) % (2 * BA) == iota((cells, 2 * BA), 1)
    count = jnp.sum(jnp.where(here, spread, 0.0), axis=1, keepdims=True)
    scale = jnp.where(count > 0.0, 1.0, 0.0) / jnp.maximum(count, 1.0)
    feats = (pillars[...].astype(F32).reshape(cells, CL) * scale).astype(BF16)
    goal = iota((BA * BR, cells), 0)
    origin = iota((BA * BR, cells), 1)
    base = (goal % BR) * (4 * BA) + (goal // BR) * 2
    total = None
    for offset in range(4):
        step = (offset // 2) * 2 * BA + offset % 2
        chosen = dot((base + step == origin).astype(F32).astype(BF16), feats).astype(BF16)
        part = dot(chosen, lidar[offset])
        total = part if total is None else total + part
    lid = jnp.maximum(total, 0.0).astype(BF16)
    for pair in range(2):
        top = pair * 2 * BR
        side[BA + pair] = jnp.concatenate(
            [lid[top : top + BR], lid[top + BR : top + 2 * BR]], axis=1
        )


def prepare_kernel(
    me_ref, image, weights, depth_hbm, bins_hbm, pillars_hbm, counts_hbm, lidar_hbm,
    cotangent_hbm,
    padded, held, spread, depth_pad, masks, slot_out, side,
    depth, bins, pillars, counts, lidar, cotangent, flat, sems,
):
    copies = [
        pltpu.make_async_copy(source, target, sems.at[index])
        for index, (source, target) in enumerate(
            [
                (depth_hbm, depth),
                (bins_hbm, bins),
                (pillars_hbm, pillars),
                (counts_hbm, counts),
                (lidar_hbm, lidar),
                (cotangent_hbm, cotangent),
                (image, padded.at[pl.ds(1, ROWS), pl.ds(0, COLS)]),
                (weights.at[0], held),
            ]
        )
    ]
    for copy in copies:
        copy.start()
    padded[0] = jnp.zeros((WIDE, C), BF16)
    padded[ROWS + 1] = jnp.zeros((WIDE, C), BF16)
    fill_spread(spread)
    for copy in copies[:6]:
        copy.wait()
    depth_pad[BINS - 6 :, :] = jnp.zeros((LANES - BINS + 6, C), BF16)
    depth_pad[0:BINS, :] = depth[...]
    fill_side(side, pillars, counts, lidar, cotangent, flat)
    cells = bins[...]
    sector = cells // (BR * BA)
    step = sector - me_ref[0] + 1
    step = jnp.where(step < 0, step + 256, step)
    step = jnp.where(step > 255, step - 256, step)
    slot_out[...] = jnp.full((COLS, LANES), -1, jnp.int32)
    slot_out[:, 0:BINS] = step * BA + cells % BA
    slot_map = slot_out[...]
    for index in range(SLOTS):
        masks[index] = (slot_map == index).astype(F32).astype(BF16)
    for copy in copies[6:]:
        copy.wait()


def prepare(*operands):
    return pl.pallas_call(
        prepare_kernel,
        out_shape=(
            jax.ShapeDtypeStruct((ROWS + 2, WIDE, C), BF16),
            jax.ShapeDtypeStruct((9, C, C), BF16),
            jax.ShapeDtypeStruct((SLOTS * LANES, WIN * BR), BF16),
            jax.ShapeDtypeStruct((LANES, C), BF16),
            jax.ShapeDtypeStruct((SLOTS, COLS, LANES), BF16),
            jax.ShapeDtypeStruct((COLS, LANES), jnp.int32),
            jax.ShapeDtypeStruct((6, BR, C), BF16),
        ),
        in_specs=[whole(pltpu.SMEM)] + [whole(pltpu.HBM)] * 8,
        out_specs=(whole(),) * 7,
        scratch_shapes=[
            pltpu.VMEM((BINS, C), BF16),
            pltpu.VMEM((COLS, BINS), jnp.int32),
            pltpu.VMEM((2 * BR, 2 * BA, CL), BF16),
            pltpu.VMEM((2 * BA, 2 * BR), jnp.int32),
            pltpu.VMEM((4, CL, CL), BF16),
            pltpu.VMEM((BR, BA, C), BF16),
            pltpu.VMEM((BR * BA, C), F32),
            pltpu.SemaphoreType.DMA((8,)),
        ],
        compiler_params=pltpu.CompilerParams(vmem_limit_bytes=24 * 2**20),
        cost_estimate=pl.CostEstimate(flops=10**8, bytes_accessed=8 * 2**20, transcendentals=0),
        name="prepare",
    )(*operands)


def front_kernel(
    me_ref, padded_in, crossed, beside, held_first, depth_pad, spread, masks, side,
    weights, merging,
    first, feat_out, share_out, lifted_out, beside_out, across_out, edge_out, probs_out,
    gain_out, merge_held,
    second, held_rest, sems,
):
    copies = [
        pltpu.make_async_copy(weights.at[1], held_rest.at[0], sems.at[0]),
        pltpu.make_async_copy(weights.at[2], held_rest.at[1], sems.at[1]),
        pltpu.make_async_copy(merging, merge_held, sems.at[2]),
    ]
    for copy in copies:
        copy.start()
    odd = lax.rem(me_ref[0], 2)
    second[0] = jnp.zeros((WIDE, C), BF16)
    second[ROWS + 1] = jnp.zeros((WIDE, C), BF16)

    def put_halo(right, left):
        first[1 : ROWS + 1, COLS:WIDE, :] = jnp.concatenate(
            [right[...].astype(F32), left[...].astype(F32)], axis=1
        ).astype(BF16)

    @pl.when(odd == 1)
    def _():
        put_halo(crossed, beside)

    @pl.when(odd == 0)
    def _():
        put_halo(beside, crossed)


    def convolved(source, held, top, narrow):
        lhs = jnp.concatenate(
            [
                source[pl.ds(top + down, BLOCK)].reshape(BLOCK * WIDE, C)
                for down in range(3)
            ],
            axis=1,
        )
        out = None
        for right in (1, 0, 2):
            kernel = jnp.concatenate(
                [held[3 * down + right] for down in range(3)], axis=0
            )
            if narrow and right == 1:
                part = dot(
                    lhs.reshape(BLOCK, WIDE, 3 * C)[:, 0:COLS].reshape(BLOCK * COLS, 3 * C),
                    kernel,
                ).reshape(BLOCK, COLS, C)
            else:
                part = dot(lhs, kernel).reshape(BLOCK, WIDE, C)
                if right != 1:
                    part = pltpu.roll(part, (1 - right) % WIDE, 1)
                if narrow:
                    part = part[:, 0:COLS]
            out = part if out is None else out + part
        return jnp.maximum(out, 0.0).astype(BF16)

    for index, (source, target) in enumerate([(first, second), (second, first)]):
        if index == 1:
            copies[0].wait()
        held = held_first if index == 0 else held_rest.at[0]
        for block in range(ROWS // BLOCK):
            target[block * BLOCK + 1 : (block + 1) * BLOCK + 1] = convolved(
                source, held, block * BLOCK, False
            )
    copies[1].wait()
    for block in range(ROWS // BLOCK):
        feat_out[block * BLOCK * COLS : (block + 1) * BLOCK * COLS, :] = convolved(
            first, held_rest.at[1], block * BLOCK, True
        ).reshape(BLOCK * COLS, C)

    lane_ok = iota((TILE, LANES), 1) < BINS

    @pl.loop(0, ROWS // TILE_H, unroll=UNROLL)
    def _(tile):
        rows = pl.ds(pl.multiple_of(tile * TILE, TILE), TILE)
        logits = nt_dot(feat_out[rows, :], depth_pad[...])
        decay = jnp.exp(-jnp.abs(logits))
        tail = jnp.log(1.0 + decay)
        soft = jnp.maximum(logits, 0.0) + tail + 0.05
        soft = jnp.where(lane_ok, soft, 0.0)
        scale = 1.0 / jnp.sum(soft, axis=1, keepdims=True)
        probs = soft * scale
        gate = jnp.exp(jnp.minimum(logits, 0.0) - tail)
        probs_out[rows, :] = probs
        gain_out[rows, :] = gate * scale
        low = probs.astype(BF16).reshape(TILE_H, COLS, LANES)
        share_out[rows, :] = dot(
            jnp.concatenate(
                [
                    (low * masks[index][None]).reshape(TILE, LANES)
                    for index in range(SLOTS)
                ],
                axis=1,
            ),
            spread[...],
        ).astype(BF16)

    lifted = tn_dot(share_out[...], feat_out[...])
    lifted_out[...] = lifted
    copies[2].wait()
    low = lifted[2 * BR : 8 * BR].reshape(6, BR, C)
    high = lifted[8 * BR : 14 * BR].reshape(6, BR, C)

    @pl.when(odd == 1)
    def _():
        beside_out[0:6] = low.astype(BF16)
        beside_out[6] = side[0]
        beside_out[7] = side[BA]
        across_out[...] = high
        edge_out[0] = side[BA - 1]
        edge_out[1] = side[BA + 1]

    @pl.when(odd == 0)
    def _():
        beside_out[0:6] = high.astype(BF16)
        beside_out[6] = side[BA - 1]
        beside_out[7] = side[BA + 1]
        across_out[...] = low
        edge_out[0] = side[0]
        edge_out[1] = side[BA]


def front(*operands):
    total = ROWS * COLS
    return pl.pallas_call(
        front_kernel,
        out_shape=(
            jax.ShapeDtypeStruct((ROWS + 2, WIDE, C), BF16),
            jax.ShapeDtypeStruct((total, C), BF16),
            jax.ShapeDtypeStruct((total, WIN * BR), BF16),
            jax.ShapeDtypeStruct((WIN * BR, C), F32),
            jax.ShapeDtypeStruct((8, BR, C), BF16),
            jax.ShapeDtypeStruct((6, BR, C), F32),
            jax.ShapeDtypeStruct((2, BR, C), BF16),
            jax.ShapeDtypeStruct((total, LANES), F32),
            jax.ShapeDtypeStruct((total, LANES), F32),
            jax.ShapeDtypeStruct((9, C + CL, C), BF16),
        ),
        in_specs=[whole(pltpu.SMEM)] + [whole()] * 8 + [whole(pltpu.HBM)] * 2,
        out_specs=(whole(),) * 10,
        scratch_shapes=[
            pltpu.VMEM((ROWS + 2, WIDE, C), BF16),
            pltpu.VMEM((LAYERS - 1, 9, C, C), BF16),
            pltpu.SemaphoreType.DMA((3,)),
        ],
        input_output_aliases={1: 0},
        compiler_params=pltpu.CompilerParams(vmem_limit_bytes=32 * 2**20),
        name="front",
    )(*operands)


def along_cycles(part, down):
    if down == 0:
        return part
    cycle = iota(part.shape, 1)
    moved = pltpu.roll(part, down % BR, 1)
    keep = cycle >= 1 if down == 1 else cycle < BR - 1
    return jnp.where(keep, moved, 0.0)


def middle_kernel(
    me_ref, lifted, side, partner, crossed, relayed, weights,
    merged_out, lid_out, table_out,
    cam, cot, lid,
):
    def put_lid(at, packed):
        lid[at] = packed[:, 0:CL]
        lid[at + 1] = packed[:, CL:]

    cam[...] = lifted[4 * BR : 12 * BR].reshape(2 * BA, BR, C)
    cot[1 : 1 + BA] = side[0:BA]
    put_lid(2, side[BA])
    put_lid(4, side[BA + 1])
    odd = lax.rem(me_ref[0], 2)

    def gather(left, right, at):
        cam[2:8] += right[0:6].astype(F32)
        cam[0:6] += left[0:6].astype(F32)
        cam[at : at + 2] += relayed[...].astype(F32)
        cot[0] = left[6]
        cot[BA + 1] = right[6]
        put_lid(0, left[7])
        put_lid(6, right[7])

    @pl.when(odd == 0)
    def _():
        gather(crossed, partner, 6)

    @pl.when(odd == 1)
    def _():
        gather(partner, crossed, 0)

    span = BA + 2
    merged_in = jnp.concatenate([cam[...].astype(BF16), lid[...]], axis=2)
    joined = jnp.concatenate(
        [merged_in[right : right + span].reshape(span * BR, C + CL) for right in range(3)],
        axis=1,
    )
    pre = None
    for down in range(3):
        kernel = jnp.concatenate([weights[3 * down + right] for right in range(3)], axis=0)
        part = along_cycles(dot(joined, kernel).reshape(span, BR, C), 1 - down)
        pre = part if pre is None else pre + part
    gate = 1.0 / (1.0 + jnp.exp(-pre))
    merged = (pre * gate).astype(BF16)
    grad_pre = (
        cot[...].astype(F32) * (gate * (1.0 + pre * (1.0 - gate)))
    ).astype(BF16)
    inner = span - 2
    total = None
    for down in range(3):
        part = None
        for right in range(3):
            piece = nt_dot(
                grad_pre[2 - right : 2 - right + inner].reshape(inner * BR, C),
                weights[3 * down + right],
            )
            part = piece if part is None else part + piece
        part = along_cycles(part.reshape(inner, BR, C + CL), down - 1)
        total = part if total is None else total + part
    table_out[...] = total[:, :, 0:C].astype(BF16)
    order = iota((BR * BA, BR * BA), 0)
    source = iota((BR * BA, BR * BA), 1)
    swap = ((order % BA) * BR + order // BA == source).astype(F32).astype(BF16)
    own = merged[1 : 1 + BA].reshape(BA * BR, C)
    turned = dot(swap, own)
    for cycle in range(BR):
        merged_out[cycle] = turned[BA * cycle : BA * (cycle + 1)].astype(BF16)
    own_lid = total[:, :, C:].astype(BF16).reshape(BA * BR, CL)
    lid_out[...] = dot(swap, own_lid).astype(BF16)


def middle(*operands):
    return pl.pallas_call(
        middle_kernel,
        out_shape=(
            jax.ShapeDtypeStruct((BR, BA, C), BF16),
            jax.ShapeDtypeStruct((BR * BA, CL), BF16),
            jax.ShapeDtypeStruct((BA, BR, C), BF16),
        ),
        in_specs=[whole(pltpu.SMEM)] + [whole()] * 6,
        out_specs=(whole(),) * 3,
        scratch_shapes=[
            pltpu.VMEM((2 * BA, BR, C), F32),
            pltpu.VMEM((BA + 2, BR, C), BF16),
            pltpu.VMEM((2 * BA, BR, CL), BF16),
        ],
        compiler_params=pltpu.CompilerParams(vmem_limit_bytes=24 * 2**20),
        name="middle",
    )(*operands)


def back_kernel(
    me_ref, own_table, partner_table, across_table, feat, share, probs, gain, slots, depth_pad,
    spread,
    cam_out,
    table, wide_table,
):
    odd = lax.rem(me_ref[0], 2)
    table[0 : 2 * BR, :] = jnp.zeros((2 * BR, C), BF16)
    table[(WIN - 2) * BR :, :] = jnp.zeros((2 * BR, C), BF16)

    def put(at, value):
        table[at * BR : (at + BA) * BR, :] = value[...].reshape(BA * BR, C)

    put(REACH, own_table)

    @pl.when(odd == 0)
    def _():
        put(REACH - BA, across_table)
        put(REACH + BA, partner_table)

    @pl.when(odd == 1)
    def _():
        put(REACH - BA, partner_table)
        put(REACH + BA, across_table)

    wide_table[...] = dot(spread[...], table[...]).astype(BF16)

    @pl.loop(0, ROWS // TALL_H, unroll=True)
    def _(tile):
        rows = pl.ds(pl.multiple_of(tile * TALL, TALL), TALL)
        block = feat[rows, :]
        slot_map = slots[...]
        picked = jnp.zeros((TALL_H, COLS, LANES), F32)
        for pair in range(SLOTS // 2):
            both = nt_dot(block, wide_table[pair * 2 * LANES : (pair + 1) * 2 * LANES, :])
            for side in range(2):
                value = both[:, side * LANES : (side + 1) * LANES].reshape(
                    TALL_H, COLS, LANES
                )
                picked = jnp.where((slot_map == 2 * pair + side)[None], value, picked)
        picked = picked.reshape(TALL, LANES)
        mean = jnp.sum(picked * probs[rows, :], axis=1, keepdims=True)
        grad_logits = ((picked - mean) * gain[rows, :]).astype(BF16)
        out = dot(share[rows, :], table[...]) + dot(grad_logits, depth_pad[...])
        cam_out[pl.ds(tile * TALL_H, TALL_H)] = out.astype(BF16).reshape(TALL_H, COLS, C)


def back(*operands):
    return pl.pallas_call(
        back_kernel,
        out_shape=jax.ShapeDtypeStruct((ROWS, COLS, C), BF16),
        in_specs=[whole(pltpu.SMEM)] + [whole()] * 10,
        out_specs=whole(),
        scratch_shapes=[
            pltpu.VMEM((WIN * BR, C), BF16),
            pltpu.VMEM((SLOTS * LANES, C), BF16),
        ],
        compiler_params=pltpu.CompilerParams(vmem_limit_bytes=32 * 2**20),
        name="back",
    )(*operands)


def swapped(block, odd_step):
    count = lax.axis_size(AXES)
    route = [(i, (i + odd_step if i % 2 else i - odd_step) % count) for i in range(count)]
    return lax.ppermute(block, AXES, route)


def local(
    image_feats, cam_weights, depth_weight, ray_bins, pillar_sums, pillar_counts,
    lidar_weight, merge_weight, out_cotangent,
):
    me = lax.axis_index(AXES).astype(jnp.int32)
    odd = me % 2 == 1
    me = me.reshape(1)
    left_edge = image_feats[:, 0:HALO]
    right_edge = image_feats[:, COLS - HALO :]
    beside = swapped(jnp.where(odd, left_edge, right_edge), -1)
    across = swapped(jnp.where(odd, right_edge, left_edge), 1)
    pinned = lambda value: pltpu.with_memory_space_constraint(value, pltpu.HBM)
    image_held, held, spread, depth_pad, masks, slots, side = prepare(
        me,
        *[
            pinned(value)
            for value in (
                image_feats, cam_weights, depth_weight.T, ray_bins, pillar_sums,
                pillar_counts.T, lidar_weight, out_cotangent,
            )
        ],
    )
    _, feat, share, lifted, aside, sums, edge, probs, gain, merge_held = front(
        me, image_held, across, beside, held, depth_pad, spread, masks, side,
        pinned(cam_weights), pinned(merge_weight),
    )
    partner = swapped(aside, -1)
    four = jnp.zeros((4, BR, C), F32)
    wide = partner.astype(F32)
    added = jnp.where(
        odd,
        jnp.concatenate([wide[4:6], four], axis=0),
        jnp.concatenate([four, wide[0:2]], axis=0),
    )
    crossed = swapped(jnp.concatenate([(sums + added).astype(BF16), edge], axis=0), 1)
    relayed = swapped(jnp.where(odd, crossed[0:2], crossed[4:6]), -1)
    merged, lid_grad, own_table = middle(
        me, lifted, side, partner, crossed, relayed, merge_held
    )
    partner_table = swapped(own_table, -1)
    across_table = swapped(own_table, 1)
    cam_grad = back(
        me, own_table, partner_table, across_table, feat, share, probs, gain, slots,
        depth_pad, spread,
    )
    return merged, cam_grad, lid_grad.reshape(BR, BA, CL)


def solution(mesh):
    columns = P(None, AXES, None)
    placed = (
        columns, P(), P(), P(AXES, None), columns, P(None, AXES), P(), P(), columns,
    )
    return jax.shard_map(
        local, mesh=mesh, in_specs=placed, out_specs=(columns,) * 3, check_vma=False
    )
```

```python
import jax
import jax.numpy as jnp
from jax import lax
from jax.experimental import pallas as pl
from jax.experimental.pallas import tpu as pltpu
from jax.sharding import PartitionSpec as P

AXES = ("branch", "strip")
ROWS = 32
COLS = 64
WIDE = 72
HALO = (WIDE - COLS) // 2
C = 256
CL = 128
BINS = 118
LANES = 128
LAYERS = 3
BR = 16
BA = 4
WIN = 16
REACH = 6
SLOTS = 12
BLOCK = 16
TILE_H = 4
TILE = TILE_H * COLS
UNROLL = 4
TALL_H = 16
TALL = TALL_H * COLS
F32 = jnp.float32
BF16 = jnp.bfloat16


def whole(memory_space=pltpu.VMEM):
    return pl.BlockSpec(memory_space=memory_space)


def iota(shape, dim):
    return lax.broadcasted_iota(jnp.int32, shape, dim)


def nt_dot(lhs, rhs):
    return lax.dot_general(lhs, rhs, (((1,), (1,)), ((), ())), preferred_element_type=F32)


def tn_dot(lhs, rhs):
    return lax.dot_general(lhs, rhs, (((0,), (0,)), ((), ())), preferred_element_type=F32)


def dot(lhs, rhs):
    return jnp.dot(lhs, rhs, preferred_element_type=F32)


def fill_spread(spread):
    bin_index = iota((LANES, WIN * BR), 0)
    column = iota((LANES, WIN * BR), 1)
    for slot in range(SLOTS):
        offset = (column - (slot + 2) * BR) * BINS
        hit = (offset <= bin_index * BR) & (bin_index * BR < offset + BINS)
        spread[slot * LANES : (slot + 1) * LANES, :] = hit.astype(F32).astype(BF16)


def fill_side(side, pillars, counts, lidar, cotangent, flat):
    for cycle in range(BR):
        flat[BA * cycle : BA * (cycle + 1), :] = cotangent[cycle].astype(F32)
    order = iota((BA * BR, BR * BA), 0)
    source = iota((BA * BR, BR * BA), 1)
    swap = ((order % BR) * BA + order // BR == source).astype(F32).astype(BF16)
    side[0:BA] = dot(swap, flat[...].astype(BF16)).astype(BF16).reshape(BA, BR, C)
    cells = 4 * BR * BA
    row = iota((cells, 2 * BR), 0)
    pick = (row // (2 * BA) == iota((cells, 2 * BR), 1)).astype(F32).astype(BF16)
    spread = nt_dot(pick, counts[...].astype(F32).astype(BF16))
    here = iota((cells, 2 * BA), 0) % (2 * BA) == iota((cells, 2 * BA), 1)
    count = jnp.sum(jnp.where(here, spread, 0.0), axis=1, keepdims=True)
    scale = jnp.where(count > 0.0, 1.0, 0.0) / jnp.maximum(count, 1.0)
    feats = (pillars[...].astype(F32).reshape(cells, CL) * scale).astype(BF16)
    goal = iota((BA * BR, cells), 0)
    origin = iota((BA * BR, cells), 1)
    base = (goal % BR) * (4 * BA) + (goal // BR) * 2
    total = None
    for offset in range(4):
        step = (offset // 2) * 2 * BA + offset % 2
        chosen = dot((base + step == origin).astype(F32).astype(BF16), feats).astype(BF16)
        part = dot(chosen, lidar[offset])
        total = part if total is None else total + part
    lid = jnp.maximum(total, 0.0).astype(BF16)
    for pair in range(2):
        top = pair * 2 * BR
        side[BA + pair] = jnp.concatenate(
            [lid[top : top + BR], lid[top + BR : top + 2 * BR]], axis=1
        )


def prepare_kernel(
    me_ref, image, weights, depth_hbm, bins_hbm, pillars_hbm, counts_hbm, lidar_hbm,
    cotangent_hbm,
    padded, held, spread, depth_pad, masks, slot_out, side,
    depth, bins, pillars, counts, lidar, cotangent, flat, sems,
):
    copies = [
        pltpu.make_async_copy(source, target, sems.at[index])
        for index, (source, target) in enumerate(
            [
                (depth_hbm, depth),
                (bins_hbm, bins),
                (pillars_hbm, pillars),
                (counts_hbm, counts),
                (lidar_hbm, lidar),
                (cotangent_hbm, cotangent),
                (image, padded.at[pl.ds(1, ROWS), pl.ds(0, COLS)]),
                (weights.at[0], held),
            ]
        )
    ]
    for copy in copies:
        copy.start()
    padded[0] = jnp.zeros((WIDE, C), BF16)
    padded[ROWS + 1] = jnp.zeros((WIDE, C), BF16)
    fill_spread(spread)
    for copy in copies[:6]:
        copy.wait()
    depth_pad[BINS - 6 :, :] = jnp.zeros((LANES - BINS + 6, C), BF16)
    depth_pad[0:BINS, :] = depth[...]
    fill_side(side, pillars, counts, lidar, cotangent, flat)
    cells = bins[...]
    sector = cells // (BR * BA)
    step = sector - me_ref[0] + 1
    step = jnp.where(step < 0, step + 256, step)
    step = jnp.where(step > 255, step - 256, step)
    slot_out[...] = jnp.full((COLS, LANES), -1, jnp.int32)
    slot_out[:, 0:BINS] = step * BA + cells % BA
    slot_map = slot_out[...]
    for index in range(SLOTS):
        masks[index] = (slot_map == index).astype(F32).astype(BF16)
    for copy in copies[6:]:
        copy.wait()


def prepare(*operands):
    return pl.pallas_call(
        prepare_kernel,
        out_shape=(
            jax.ShapeDtypeStruct((ROWS + 2, WIDE, C), BF16),
            jax.ShapeDtypeStruct((9, C, C), BF16),
            jax.ShapeDtypeStruct((SLOTS * LANES, WIN * BR), BF16),
            jax.ShapeDtypeStruct((LANES, C), BF16),
            jax.ShapeDtypeStruct((SLOTS, COLS, LANES), BF16),
            jax.ShapeDtypeStruct((COLS, LANES), jnp.int32),
            jax.ShapeDtypeStruct((6, BR, C), BF16),
        ),
        in_specs=[whole(pltpu.SMEM)] + [whole(pltpu.HBM)] * 8,
        out_specs=(whole(),) * 7,
        scratch_shapes=[
            pltpu.VMEM((BINS, C), BF16),
            pltpu.VMEM((COLS, BINS), jnp.int32),
            pltpu.VMEM((2 * BR, 2 * BA, CL), BF16),
            pltpu.VMEM((2 * BA, 2 * BR), jnp.int32),
            pltpu.VMEM((4, CL, CL), BF16),
            pltpu.VMEM((BR, BA, C), BF16),
            pltpu.VMEM((BR * BA, C), F32),
            pltpu.SemaphoreType.DMA((8,)),
        ],
        compiler_params=pltpu.CompilerParams(vmem_limit_bytes=24 * 2**20),
        cost_estimate=pl.CostEstimate(flops=10**8, bytes_accessed=8 * 2**20, transcendentals=0),
        name="prepare",
    )(*operands)


def front_kernel(
    me_ref, padded_in, crossed, beside, held_first, depth_pad, spread, masks, side,
    weights, merging,
    first, feat_out, share_out, lifted_out, note_out, far_out, probs_out, gain_out, merge_held,
    second, held_rest, sems,
):
    copies = [
        pltpu.make_async_copy(weights.at[1], held_rest.at[0], sems.at[0]),
        pltpu.make_async_copy(weights.at[2], held_rest.at[1], sems.at[1]),
        pltpu.make_async_copy(merging, merge_held, sems.at[2]),
    ]
    for copy in copies:
        copy.start()
    odd = lax.rem(me_ref[0], 2)
    second[0] = jnp.zeros((WIDE, C), BF16)
    second[ROWS + 1] = jnp.zeros((WIDE, C), BF16)

    def put_halo(right, left):
        first[1 : ROWS + 1, COLS:WIDE, :] = jnp.concatenate(
            [right[...].astype(F32), left[...].astype(F32)], axis=1
        ).astype(BF16)

    @pl.when(odd == 1)
    def _():
        put_halo(crossed, beside)

    @pl.when(odd == 0)
    def _():
        put_halo(beside, crossed)

    note_out[WIN : WIN + 6] = side[...]

    def convolved(source, held, top, narrow):
        lhs = jnp.concatenate(
            [
                source[pl.ds(top + down, BLOCK)].reshape(BLOCK * WIDE, C)
                for down in range(3)
            ],
            axis=1,
        )
        out = None
        for right in (1, 0, 2):
            kernel = jnp.concatenate(
                [held[3 * down + right] for down in range(3)], axis=0
            )
            if narrow and right == 1:
                part = dot(
                    lhs.reshape(BLOCK, WIDE, 3 * C)[:, 0:COLS].reshape(BLOCK * COLS, 3 * C),
                    kernel,
                ).reshape(BLOCK, COLS, C)
            else:
                part = dot(lhs, kernel).reshape(BLOCK, WIDE, C)
                if right != 1:
                    part = pltpu.roll(part, (1 - right) % WIDE, 1)
                if narrow:
                    part = part[:, 0:COLS]
            out = part if out is None else out + part
        return jnp.maximum(out, 0.0).astype(BF16)

    for index, (source, target) in enumerate([(first, second), (second, first)]):
        if index == 1:
            copies[0].wait()
        held = held_first if index == 0 else held_rest.at[0]
        for block in range(ROWS // BLOCK):
            target[block * BLOCK + 1 : (block + 1) * BLOCK + 1] = convolved(
                source, held, block * BLOCK, False
            )
    copies[1].wait()
    for block in range(ROWS // BLOCK):
        feat_out[block * BLOCK * COLS : (block + 1) * BLOCK * COLS, :] = convolved(
            first, held_rest.at[1], block * BLOCK, True
        ).reshape(BLOCK * COLS, C)

    lane_ok = iota((TILE, LANES), 1) < BINS

    @pl.loop(0, ROWS // TILE_H, unroll=UNROLL)
    def _(tile):
        rows = pl.ds(pl.multiple_of(tile * TILE, TILE), TILE)
        logits = nt_dot(feat_out[rows, :], depth_pad[...])
        decay = jnp.exp(-jnp.abs(logits))
        tail = jnp.log(1.0 + decay)
        soft = jnp.maximum(logits, 0.0) + tail + 0.05
        soft = jnp.where(lane_ok, soft, 0.0)
        scale = 1.0 / jnp.sum(soft, axis=1, keepdims=True)
        probs = soft * scale
        gate = jnp.exp(jnp.minimum(logits, 0.0) - tail)
        probs_out[rows, :] = probs
        gain_out[rows, :] = gate * scale
        low = probs.astype(BF16).reshape(TILE_H, COLS, LANES)
        share_out[rows, :] = dot(
            jnp.concatenate(
                [
                    (low * masks[index][None]).reshape(TILE, LANES)
                    for index in range(SLOTS)
                ],
                axis=1,
            ),
            spread[...],
        ).astype(BF16)

    lifted = tn_dot(share_out[...], feat_out[...])
    lifted_out[...] = lifted
    note_out[0:WIN] = lifted.astype(BF16).reshape(WIN, BR, C)
    copies[2].wait()

    @pl.when(odd == 1)
    def _():
        far_out[...] = note_out[12:14]

    @pl.when(odd == 0)
    def _():
        far_out[...] = note_out[2:4]


def front(*operands):
    total = ROWS * COLS
    return pl.pallas_call(
        front_kernel,
        out_shape=(
            jax.ShapeDtypeStruct((ROWS + 2, WIDE, C), BF16),
            jax.ShapeDtypeStruct((total, C), BF16),
            jax.ShapeDtypeStruct((total, WIN * BR), BF16),
            jax.ShapeDtypeStruct((WIN * BR, C), F32),
            jax.ShapeDtypeStruct((WIN + 6, BR, C), BF16),
            jax.ShapeDtypeStruct((2, BR, C), BF16),
            jax.ShapeDtypeStruct((total, LANES), F32),
            jax.ShapeDtypeStruct((total, LANES), F32),
            jax.ShapeDtypeStruct((9, C + CL, C), BF16),
        ),
        in_specs=[whole(pltpu.SMEM)] + [whole()] * 8 + [whole(pltpu.HBM)] * 2,
        out_specs=(whole(),) * 9,
        scratch_shapes=[
            pltpu.VMEM((ROWS + 2, WIDE, C), BF16),
            pltpu.VMEM((LAYERS - 1, 9, C, C), BF16),
            pltpu.SemaphoreType.DMA((3,)),
        ],
        input_output_aliases={1: 0},
        compiler_params=pltpu.CompilerParams(vmem_limit_bytes=32 * 2**20),
        name="front",
    )(*operands)


def along_cycles(part, down):
    if down == 0:
        return part
    cycle = iota(part.shape, 1)
    moved = pltpu.roll(part, down % BR, 1)
    keep = cycle >= 1 if down == 1 else cycle < BR - 1
    return jnp.where(keep, moved, 0.0)


def back_kernel(
    me_ref, lifted, note, partner, crossed, relayed, far, weights, feat, share, probs, gain,
    slots, depth_pad, spread,
    merged_out, cam_out, lid_out,
    cam, cot, lid, table, wide_table,
):

    def put_lid(at, packed):
        lid[at] = packed[:, 0:CL]
        lid[at + 1] = packed[:, CL:]

    cam[...] = lifted[...].reshape(WIN, BR, C)
    cot[REACH : REACH + BA] = note[WIN : WIN + BA]
    put_lid(REACH, note[WIN + BA])
    put_lid(REACH + 2, note[WIN + BA + 1])
    cot[0] = jnp.zeros((BR, C), BF16)
    cot[WIN - 1] = jnp.zeros((BR, C), BF16)
    odd = lax.rem(me_ref[0], 2)

    def gather(low_side):
        near = 10 if low_side else 2
        other = 2 if low_side else 10
        cam[6:16] += (partner[2:12] if low_side else crossed[0:10]).astype(F32)
        cam[0:10] += (crossed[0:10] if low_side else partner[4:14]).astype(F32)
        start = 10 if low_side else 0
        cam[start : start + 6] += relayed[0:6].astype(F32)
        edge = 0 if low_side else 14
        cam[edge : edge + 2] += far[...].astype(F32)
        cot[near : near + 4] = partner[WIN : WIN + 4]
        cot[other : other + 4] = crossed[10:14]
        cot[1 if low_side else 14] = crossed[14]
        cot[14 if low_side else 1] = relayed[6]
        put_lid(near, partner[WIN + 4])
        put_lid(near + 2, partner[WIN + 5])
        put_lid(other, crossed[15])
        put_lid(other + 2, crossed[16])
        put_lid(0 if low_side else 14, crossed[17])
        put_lid(14 if low_side else 0, relayed[7])

    @pl.when(odd == 0)
    def _():
        gather(True)

    @pl.when(odd == 1)
    def _():
        gather(False)

    span = WIN - 2
    merged_in = jnp.concatenate([cam[...].astype(BF16), lid[...]], axis=2)
    joined = jnp.concatenate(
        [merged_in[right : right + span].reshape(span * BR, C + CL) for right in range(3)],
        axis=1,
    )
    pre = None
    for down in range(3):
        kernel = jnp.concatenate([weights[3 * down + right] for right in range(3)], axis=0)
        part = along_cycles(dot(joined, kernel).reshape(span, BR, C), 1 - down)
        pre = part if pre is None else pre + part
    gate = 1.0 / (1.0 + jnp.exp(-pre))
    merged = (pre * gate).astype(BF16)
    grad_pre = (
        cot[1 : WIN - 1].astype(F32) * (gate * (1.0 + pre * (1.0 - gate)))
    ).astype(BF16)
    inner = span - 2
    total = None
    for down in range(3):
        part = None
        for right in range(3):
            piece = nt_dot(
                grad_pre[2 - right : 2 - right + inner].reshape(inner * BR, C),
                weights[3 * down + right],
            )
            part = piece if part is None else part + piece
        part = along_cycles(part.reshape(inner, BR, C + CL), down - 1)
        total = part if total is None else total + part
    table[0 : 2 * BR, :] = jnp.zeros((2 * BR, C), BF16)
    table[(WIN - 2) * BR :, :] = jnp.zeros((2 * BR, C), BF16)
    table[2 * BR : (WIN - 2) * BR, :] = total[:, :, 0:C].astype(BF16).reshape(inner * BR, C)
    order = iota((BR * BA, BR * BA), 0)
    source = iota((BR * BA, BR * BA), 1)
    swap = ((order % BA) * BR + order // BA == source).astype(F32).astype(BF16)
    own = merged[REACH - 1 : REACH - 1 + BA].reshape(BA * BR, C)
    turned = dot(swap, own)
    for cycle in range(BR):
        merged_out[cycle] = turned[BA * cycle : BA * (cycle + 1)].astype(BF16)
    own_lid = total[REACH - 2 : REACH - 2 + BA, :, C:].astype(BF16).reshape(BA * BR, CL)
    lid_out[...] = dot(swap, own_lid).astype(BF16)
    wide_table[...] = dot(spread[...], table[...]).astype(BF16)

    @pl.loop(0, ROWS // TALL_H, unroll=True)
    def _(tile):
        rows = pl.ds(pl.multiple_of(tile * TALL, TALL), TALL)
        block = feat[rows, :]
        slot_map = slots[...]
        picked = jnp.zeros((TALL_H, COLS, LANES), F32)
        for pair in range(SLOTS // 2):
            both = nt_dot(block, wide_table[pair * 2 * LANES : (pair + 1) * 2 * LANES, :])
            for side in range(2):
                value = both[:, side * LANES : (side + 1) * LANES].reshape(
                    TALL_H, COLS, LANES
                )
                picked = jnp.where((slot_map == 2 * pair + side)[None], value, picked)
        picked = picked.reshape(TALL, LANES)
        mean = jnp.sum(picked * probs[rows, :], axis=1, keepdims=True)
        grad_logits = ((picked - mean) * gain[rows, :]).astype(BF16)
        out = dot(share[rows, :], table[...]) + dot(grad_logits, depth_pad[...])
        cam_out[pl.ds(tile * TALL_H, TALL_H)] = out.astype(BF16).reshape(TALL_H, COLS, C)


def back(*operands):
    return pl.pallas_call(
        back_kernel,
        out_shape=(
            jax.ShapeDtypeStruct((BR, BA, C), BF16),
            jax.ShapeDtypeStruct((ROWS, COLS, C), BF16),
            jax.ShapeDtypeStruct((BR * BA, CL), BF16),
        ),
        in_specs=[whole(pltpu.SMEM)] + [whole()] * 14,
        out_specs=(whole(),) * 3,
        scratch_shapes=[
            pltpu.VMEM((WIN, BR, C), F32),
            pltpu.VMEM((WIN, BR, C), BF16),
            pltpu.VMEM((WIN, BR, CL), BF16),
            pltpu.VMEM((WIN * BR, C), BF16),
            pltpu.VMEM((SLOTS * LANES, C), BF16),
        ],
        compiler_params=pltpu.CompilerParams(vmem_limit_bytes=32 * 2**20),
        name="back",
    )(*operands)


def swapped(block, odd_step):
    count = lax.axis_size(AXES)
    route = [(i, (i + odd_step if i % 2 else i - odd_step) % count) for i in range(count)]
    return lax.ppermute(block, AXES, route)


def local(
    image_feats, cam_weights, depth_weight, ray_bins, pillar_sums, pillar_counts,
    lidar_weight, merge_weight, out_cotangent,
):
    me = lax.axis_index(AXES).astype(jnp.int32)
    odd = me % 2 == 1
    me = me.reshape(1)
    left_edge = image_feats[:, 0:HALO]
    right_edge = image_feats[:, COLS - HALO :]
    beside = swapped(jnp.where(odd, left_edge, right_edge), -1)
    across = swapped(jnp.where(odd, right_edge, left_edge), 1)
    pinned = lambda value: pltpu.with_memory_space_constraint(value, pltpu.HBM)
    padded, held, spread, depth_pad, masks, slots, side = prepare(
        me,
        *[
            pinned(value)
            for value in (
                image_feats, cam_weights, depth_weight.T, ray_bins, pillar_sums,
                pillar_counts.T, lidar_weight, out_cotangent,
            )
        ],
    )
    _, feat, share, lifted, note, far, probs, gain, merge_held = front(
        me, padded, across, beside, held, depth_pad, spread, masks, side,
        pinned(cam_weights), pinned(merge_weight),
    )
    partner = swapped(note, -1)
    far_got = swapped(far, 3)
    wide = lambda a: a.astype(F32)
    four = jnp.zeros((4, BR, C), F32)
    mine = lifted.reshape(WIN, BR, C)
    rise = mine[2:12] + jnp.concatenate([four, wide(partner[2:8])], 0)
    fall = mine[4:14] + jnp.concatenate([wide(partner[8:14]), four], 0)
    crossing = jnp.concatenate(
        [
            jnp.where(odd, fall, rise).astype(BF16),
            note[16:20],
            jnp.where(odd, partner[19:20], partner[16:17]),
            note[20:22],
            jnp.where(odd, partner[21:22], partner[20:21]),
        ],
        axis=0,
    )
    crossed = swapped(crossing, 1)
    relay = jnp.concatenate(
        [
            jnp.where(odd, crossed[0:6], crossed[4:10]),
            jnp.where(odd, crossed[10:11], crossed[13:14]),
            jnp.where(odd, crossed[15:16], crossed[16:17]),
        ],
        axis=0,
    )
    relay, far_got = lax.optimization_barrier((relay, far_got))
    relayed = swapped(relay, -1)
    merged, cam_grad, lid_grad = back(
        me, lifted, note, partner, crossed, relayed, far_got, merge_held, feat, share,
        probs, gain, slots, depth_pad, spread,
    )
    return merged, cam_grad, lid_grad.reshape(BR, BA, CL)


def solution(mesh):
    columns = P(None, AXES, None)
    placed = (
        columns, P(), P(), P(AXES, None), columns, P(None, AXES), P(), P(), columns,
    )
    return jax.shard_map(
        local, mesh=mesh, in_specs=placed, out_specs=(columns,) * 3, check_vma=False
    )
```

```python
import jax
import jax.numpy as jnp
from jax import lax
from jax.experimental import pallas as pl
from jax.experimental.pallas import tpu as pltpu
from jax.sharding import PartitionSpec as P

AXES = ("branch", "strip")
ROWS = 32
COLS = 64
WIDE = 72
HALO = (WIDE - COLS) // 2
C = 256
CL = 128
BINS = 118
LANES = 128
LAYERS = 3
BR = 16
BA = 4
WIN = 16
REACH = 6
SLOTS = 12
BLOCK = 16
TILE_H = 4
TILE = TILE_H * COLS
UNROLL = 4
TALL_H = 16
TALL = TALL_H * COLS
F32 = jnp.float32
BF16 = jnp.bfloat16


def whole(memory_space=pltpu.VMEM):
    return pl.BlockSpec(memory_space=memory_space)


def iota(shape, dim):
    return lax.broadcasted_iota(jnp.int32, shape, dim)


def nt_dot(lhs, rhs):
    return lax.dot_general(lhs, rhs, (((1,), (1,)), ((), ())), preferred_element_type=F32)


def tn_dot(lhs, rhs):
    return lax.dot_general(lhs, rhs, (((0,), (0,)), ((), ())), preferred_element_type=F32)


def dot(lhs, rhs):
    return jnp.dot(lhs, rhs, preferred_element_type=F32)


def fill_spread(spread):
    bin_index = iota((LANES, WIN * BR), 0)
    column = iota((LANES, WIN * BR), 1)
    for slot in range(SLOTS):
        offset = (column - (slot + 2) * BR) * BINS
        hit = (offset <= bin_index * BR) & (bin_index * BR < offset + BINS)
        spread[slot * LANES : (slot + 1) * LANES, :] = hit.astype(F32).astype(BF16)


def fill_side(side, pillars, counts, lidar, cotangent, flat):
    for cycle in range(BR):
        flat[BA * cycle : BA * (cycle + 1), :] = cotangent[cycle].astype(F32)
    order = iota((BA * BR, BR * BA), 0)
    source = iota((BA * BR, BR * BA), 1)
    swap = ((order % BR) * BA + order // BR == source).astype(F32).astype(BF16)
    side[0:BA] = dot(swap, flat[...].astype(BF16)).astype(BF16).reshape(BA, BR, C)
    cells = 4 * BR * BA
    row = iota((cells, 2 * BR), 0)
    pick = (row // (2 * BA) == iota((cells, 2 * BR), 1)).astype(F32).astype(BF16)
    spread = nt_dot(pick, counts[...].astype(F32).astype(BF16))
    here = iota((cells, 2 * BA), 0) % (2 * BA) == iota((cells, 2 * BA), 1)
    count = jnp.sum(jnp.where(here, spread, 0.0), axis=1, keepdims=True)
    scale = jnp.where(count > 0.0, 1.0, 0.0) / jnp.maximum(count, 1.0)
    feats = (pillars[...].astype(F32).reshape(cells, CL) * scale).astype(BF16)
    goal = iota((BA * BR, cells), 0)
    origin = iota((BA * BR, cells), 1)
    base = (goal % BR) * (4 * BA) + (goal // BR) * 2
    total = None
    for offset in range(4):
        step = (offset // 2) * 2 * BA + offset % 2
        chosen = dot((base + step == origin).astype(F32).astype(BF16), feats).astype(BF16)
        part = dot(chosen, lidar[offset])
        total = part if total is None else total + part
    lid = jnp.maximum(total, 0.0).astype(BF16)
    for pair in range(2):
        top = pair * 2 * BR
        side[BA + pair] = jnp.concatenate(
            [lid[top : top + BR], lid[top + BR : top + 2 * BR]], axis=1
        )


def prepare_kernel(
    me_ref, image, weights, depth_hbm, bins_hbm, pillars_hbm, counts_hbm, lidar_hbm,
    cotangent_hbm,
    padded, held, spread, depth_pad, masks, slot_out, side,
    depth, bins, pillars, counts, lidar, cotangent, flat, sems,
):
    copies = [
        pltpu.make_async_copy(source, target, sems.at[index])
        for index, (source, target) in enumerate(
            [
                (depth_hbm, depth),
                (bins_hbm, bins),
                (pillars_hbm, pillars),
                (counts_hbm, counts),
                (lidar_hbm, lidar),
                (cotangent_hbm, cotangent),
                (image, padded.at[pl.ds(1, ROWS), pl.ds(0, COLS)]),
                (weights.at[0], held),
            ]
        )
    ]
    for copy in copies:
        copy.start()
    padded[0] = jnp.zeros((WIDE, C), BF16)
    padded[ROWS + 1] = jnp.zeros((WIDE, C), BF16)
    fill_spread(spread)
    for copy in copies[:6]:
        copy.wait()
    depth_pad[BINS - 6 :, :] = jnp.zeros((LANES - BINS + 6, C), BF16)
    depth_pad[0:BINS, :] = depth[...]
    fill_side(side, pillars, counts, lidar, cotangent, flat)
    cells = bins[...]
    sector = cells // (BR * BA)
    step = sector - me_ref[0] + 1
    step = jnp.where(step < 0, step + 256, step)
    step = jnp.where(step > 255, step - 256, step)
    slot_out[...] = jnp.full((COLS, LANES), -1, jnp.int32)
    slot_out[:, 0:BINS] = step * BA + cells % BA
    slot_map = slot_out[...]
    for index in range(SLOTS):
        masks[index] = (slot_map == index).astype(F32).astype(BF16)
    for copy in copies[6:]:
        copy.wait()


def prepare(*operands):
    return pl.pallas_call(
        prepare_kernel,
        out_shape=(
            jax.ShapeDtypeStruct((ROWS + 2, WIDE, C), BF16),
            jax.ShapeDtypeStruct((9, C, C), BF16),
            jax.ShapeDtypeStruct((SLOTS * LANES, WIN * BR), BF16),
            jax.ShapeDtypeStruct((LANES, C), BF16),
            jax.ShapeDtypeStruct((SLOTS, COLS, LANES), BF16),
            jax.ShapeDtypeStruct((COLS, LANES), jnp.int32),
            jax.ShapeDtypeStruct((6, BR, C), BF16),
        ),
        in_specs=[whole(pltpu.SMEM)] + [whole(pltpu.HBM)] * 8,
        out_specs=(whole(),) * 7,
        scratch_shapes=[
            pltpu.VMEM((BINS, C), BF16),
            pltpu.VMEM((COLS, BINS), jnp.int32),
            pltpu.VMEM((2 * BR, 2 * BA, CL), BF16),
            pltpu.VMEM((2 * BA, 2 * BR), jnp.int32),
            pltpu.VMEM((4, CL, CL), BF16),
            pltpu.VMEM((BR, BA, C), BF16),
            pltpu.VMEM((BR * BA, C), F32),
            pltpu.SemaphoreType.DMA((8,)),
        ],
        compiler_params=pltpu.CompilerParams(vmem_limit_bytes=24 * 2**20),
        cost_estimate=pl.CostEstimate(flops=10**8, bytes_accessed=8 * 2**20, transcendentals=0),
        name="prepare",
    )(*operands)


def front_kernel(
    me_ref, padded_in, crossed, beside, held_first, depth_pad, spread, masks, side,
    weights, merging,
    first, feat_out, share_out, lifted_out, note_out, far_out, probs_out, gain_out, merge_held,
    second, held_rest, sems,
):
    copies = [
        pltpu.make_async_copy(weights.at[1], held_rest.at[0], sems.at[0]),
        pltpu.make_async_copy(weights.at[2], held_rest.at[1], sems.at[1]),
        pltpu.make_async_copy(merging, merge_held, sems.at[2]),
    ]
    for copy in copies:
        copy.start()
    odd = lax.rem(me_ref[0], 2)
    second[0] = jnp.zeros((WIDE, C), BF16)
    second[ROWS + 1] = jnp.zeros((WIDE, C), BF16)

    def put_halo(right, left):
        first[1 : ROWS + 1, COLS:WIDE, :] = jnp.concatenate(
            [right[...].astype(F32), left[...].astype(F32)], axis=1
        ).astype(BF16)

    @pl.when(odd == 1)
    def _():
        put_halo(crossed, beside)

    @pl.when(odd == 0)
    def _():
        put_halo(beside, crossed)

    note_out[WIN : WIN + 6] = side[...]

    def convolved(source, held, top, narrow):
        lhs = jnp.concatenate(
            [
                source[pl.ds(top + down, BLOCK)].reshape(BLOCK * WIDE, C)
                for down in range(3)
            ],
            axis=1,
        )
        out = None
        for right in (1, 0, 2):
            kernel = jnp.concatenate(
                [held[3 * down + right] for down in range(3)], axis=0
            )
            if narrow and right == 1:
                part = dot(
                    lhs.reshape(BLOCK, WIDE, 3 * C)[:, 0:COLS].reshape(BLOCK * COLS, 3 * C),
                    kernel,
                ).reshape(BLOCK, COLS, C)
            else:
                part = dot(lhs, kernel).reshape(BLOCK, WIDE, C)
                if right != 1:
                    part = pltpu.roll(part, (1 - right) % WIDE, 1)
                if narrow:
                    part = part[:, 0:COLS]
            out = part if out is None else out + part
        return jnp.maximum(out, 0.0).astype(BF16)

    for index, (source, target) in enumerate([(first, second), (second, first)]):
        if index == 1:
            copies[0].wait()
        held = held_first if index == 0 else held_rest.at[0]
        for block in range(ROWS // BLOCK):
            target[block * BLOCK + 1 : (block + 1) * BLOCK + 1] = convolved(
                source, held, block * BLOCK, False
            )
    copies[1].wait()
    for block in range(ROWS // BLOCK):
        feat_out[block * BLOCK * COLS : (block + 1) * BLOCK * COLS, :] = convolved(
            first, held_rest.at[1], block * BLOCK, True
        ).reshape(BLOCK * COLS, C)

    lane_ok = iota((TILE, LANES), 1) < BINS

    @pl.loop(0, ROWS // TILE_H, unroll=UNROLL)
    def _(tile):
        rows = pl.ds(pl.multiple_of(tile * TILE, TILE), TILE)
        logits = nt_dot(feat_out[rows, :], depth_pad[...])
        decay = jnp.exp(-jnp.abs(logits))
        tail = jnp.log(1.0 + decay)
        soft = jnp.maximum(logits, 0.0) + tail + 0.05
        soft = jnp.where(lane_ok, soft, 0.0)
        scale = 1.0 / jnp.sum(soft, axis=1, keepdims=True)
        probs = soft * scale
        gate = jnp.exp(jnp.minimum(logits, 0.0) - tail)
        probs_out[rows, :] = probs
        gain_out[rows, :] = gate * scale
        low = probs.astype(BF16).reshape(TILE_H, COLS, LANES)
        share_out[rows, :] = dot(
            jnp.concatenate(
                [
                    (low * masks[index][None]).reshape(TILE, LANES)
                    for index in range(SLOTS)
                ],
                axis=1,
            ),
            spread[...],
        ).astype(BF16)

    lifted = tn_dot(share_out[...], feat_out[...])
    lifted_out[...] = lifted
    note_out[0:WIN] = lifted.astype(BF16).reshape(WIN, BR, C)
    copies[2].wait()

    @pl.when(odd == 1)
    def _():
        far_out[...] = note_out[12:14]

    @pl.when(odd == 0)
    def _():
        far_out[...] = note_out[2:4]


def front(*operands):
    total = ROWS * COLS
    return pl.pallas_call(
        front_kernel,
        out_shape=(
            jax.ShapeDtypeStruct((ROWS + 2, WIDE, C), BF16),
            jax.ShapeDtypeStruct((total, C), BF16),
            jax.ShapeDtypeStruct((total, WIN * BR), BF16),
            jax.ShapeDtypeStruct((WIN * BR, C), F32),
            jax.ShapeDtypeStruct((WIN + 6, BR, C), BF16),
            jax.ShapeDtypeStruct((2, BR, C), BF16),
            jax.ShapeDtypeStruct((total, LANES), F32),
            jax.ShapeDtypeStruct((total, LANES), F32),
            jax.ShapeDtypeStruct((9, C + CL, C), BF16),
        ),
        in_specs=[whole(pltpu.SMEM)] + [whole()] * 8 + [whole(pltpu.HBM)] * 2,
        out_specs=(whole(),) * 9,
        scratch_shapes=[
            pltpu.VMEM((ROWS + 2, WIDE, C), BF16),
            pltpu.VMEM((LAYERS - 1, 9, C, C), BF16),
            pltpu.SemaphoreType.DMA((3,)),
        ],
        input_output_aliases={1: 0},
        compiler_params=pltpu.CompilerParams(vmem_limit_bytes=32 * 2**20),
        name="front",
    )(*operands)


def along_cycles(part, down):
    if down == 0:
        return part
    cycle = iota(part.shape, 1)
    moved = pltpu.roll(part, down % BR, 1)
    keep = cycle >= 1 if down == 1 else cycle < BR - 1
    return jnp.where(keep, moved, 0.0)


def back_kernel(
    me_ref, lifted, note, partner, crossed, relayed, far, weights, feat, share, probs, gain,
    slots, depth_pad, spread,
    merged_out, cam_out, lid_out,
    cam, cot, lid, table, wide_table,
):

    def put_lid(at, packed):
        lid[at] = packed[:, 0:CL]
        lid[at + 1] = packed[:, CL:]

    cam[...] = lifted[...].reshape(WIN, BR, C)
    cot[REACH : REACH + BA] = note[WIN : WIN + BA]
    put_lid(REACH, note[WIN + BA])
    put_lid(REACH + 2, note[WIN + BA + 1])
    cot[0] = jnp.zeros((BR, C), BF16)
    cot[WIN - 1] = jnp.zeros((BR, C), BF16)
    odd = lax.rem(me_ref[0], 2)

    def gather(low_side):
        near = 10 if low_side else 2
        other = 2 if low_side else 10
        cam[6:16] += (partner[2:12] if low_side else crossed[0:10]).astype(F32)
        cam[0:10] += (crossed[0:10] if low_side else partner[4:14]).astype(F32)
        start = 10 if low_side else 0
        cam[start : start + 6] += relayed[0:6].astype(F32)
        edge = 0 if low_side else 14
        cam[edge : edge + 2] += far[...].astype(F32)
        cot[near : near + 4] = partner[WIN : WIN + 4]
        cot[other : other + 4] = crossed[10:14]
        cot[1 if low_side else 14] = crossed[14]
        cot[14 if low_side else 1] = relayed[6]
        put_lid(near, partner[WIN + 4])
        put_lid(near + 2, partner[WIN + 5])
        put_lid(other, crossed[15])
        put_lid(other + 2, crossed[16])
        put_lid(0 if low_side else 14, crossed[17])
        put_lid(14 if low_side else 0, relayed[7])

    @pl.when(odd == 0)
    def _():
        gather(True)

    @pl.when(odd == 1)
    def _():
        gather(False)

    span = WIN - 2
    merged_in = jnp.concatenate([cam[...].astype(BF16), lid[...]], axis=2)
    joined = jnp.concatenate(
        [merged_in[right : right + span].reshape(span * BR, C + CL) for right in range(3)],
        axis=1,
    )
    pre = None
    for down in range(3):
        kernel = jnp.concatenate([weights[3 * down + right] for right in range(3)], axis=0)
        part = along_cycles(dot(joined, kernel).reshape(span, BR, C), 1 - down)
        pre = part if pre is None else pre + part
    gate = 1.0 / (1.0 + jnp.exp(-pre))
    merged = (pre * gate).astype(BF16)
    grad_pre = (
        cot[1 : WIN - 1].astype(F32) * (gate * (1.0 + pre * (1.0 - gate)))
    ).astype(BF16)
    inner = span - 2
    total = None
    for down in range(3):
        part = None
        for right in range(3):
            piece = nt_dot(
                grad_pre[2 - right : 2 - right + inner].reshape(inner * BR, C),
                weights[3 * down + right],
            )
            part = piece if part is None else part + piece
        part = along_cycles(part.reshape(inner, BR, C + CL), down - 1)
        total = part if total is None else total + part
    table[0 : 2 * BR, :] = jnp.zeros((2 * BR, C), BF16)
    table[(WIN - 2) * BR :, :] = jnp.zeros((2 * BR, C), BF16)
    table[2 * BR : (WIN - 2) * BR, :] = total[:, :, 0:C].astype(BF16).reshape(inner * BR, C)
    order = iota((BR * BA, BR * BA), 0)
    source = iota((BR * BA, BR * BA), 1)
    swap = ((order % BA) * BR + order // BA == source).astype(F32).astype(BF16)
    own = merged[REACH - 1 : REACH - 1 + BA].reshape(BA * BR, C)
    turned = dot(swap, own)
    for cycle in range(BR):
        merged_out[cycle] = turned[BA * cycle : BA * (cycle + 1)].astype(BF16)
    own_lid = total[REACH - 2 : REACH - 2 + BA, :, C:].astype(BF16).reshape(BA * BR, CL)
    lid_out[...] = dot(swap, own_lid).astype(BF16)
    wide_table[...] = dot(spread[...], table[...]).astype(BF16)

    @pl.loop(0, ROWS // TALL_H, unroll=True)
    def _(tile):
        rows = pl.ds(pl.multiple_of(tile * TALL, TALL), TALL)
        block = feat[rows, :]
        slot_map = slots[...]
        picked = jnp.zeros((TALL_H, COLS, LANES), F32)
        for pair in range(SLOTS // 2):
            both = nt_dot(block, wide_table[pair * 2 * LANES : (pair + 1) * 2 * LANES, :])
            for side in range(2):
                value = both[:, side * LANES : (side + 1) * LANES].reshape(
                    TALL_H, COLS, LANES
                )
                picked = jnp.where((slot_map == 2 * pair + side)[None], value, picked)
        picked = picked.reshape(TALL, LANES)
        mean = jnp.sum(picked * probs[rows, :], axis=1, keepdims=True)
        grad_logits = ((picked - mean) * gain[rows, :]).astype(BF16)
        out = dot(share[rows, :], table[...]) + dot(grad_logits, depth_pad[...])
        cam_out[pl.ds(tile * TALL_H, TALL_H)] = out.astype(BF16).reshape(TALL_H, COLS, C)


def back(*operands):
    return pl.pallas_call(
        back_kernel,
        out_shape=(
            jax.ShapeDtypeStruct((BR, BA, C), BF16),
            jax.ShapeDtypeStruct((ROWS, COLS, C), BF16),
            jax.ShapeDtypeStruct((BR * BA, CL), BF16),
        ),
        in_specs=[whole(pltpu.SMEM)] + [whole()] * 14,
        out_specs=(whole(),) * 3,
        scratch_shapes=[
            pltpu.VMEM((WIN, BR, C), F32),
            pltpu.VMEM((WIN, BR, C), BF16),
            pltpu.VMEM((WIN, BR, CL), BF16),
            pltpu.VMEM((WIN * BR, C), BF16),
            pltpu.VMEM((SLOTS * LANES, C), BF16),
        ],
        compiler_params=pltpu.CompilerParams(vmem_limit_bytes=32 * 2**20),
        name="back",
    )(*operands)


def swapped(block, odd_step):
    count = lax.axis_size(AXES)
    route = [(i, (i + odd_step if i % 2 else i - odd_step) % count) for i in range(count)]
    return lax.ppermute(block, AXES, route)


def local(
    image_feats, cam_weights, depth_weight, ray_bins, pillar_sums, pillar_counts,
    lidar_weight, merge_weight, out_cotangent,
):
    me = lax.axis_index(AXES).astype(jnp.int32)
    odd = me % 2 == 1
    me = me.reshape(1)
    left_edge = image_feats[:, 0:HALO]
    right_edge = image_feats[:, COLS - HALO :]
    beside = swapped(jnp.where(odd, left_edge, right_edge), -1)
    across = swapped(jnp.where(odd, right_edge, left_edge), 1)
    pinned = lambda value: pltpu.with_memory_space_constraint(value, pltpu.HBM)
    padded, held, spread, depth_pad, masks, slots, side = prepare(
        me,
        *[
            pinned(value)
            for value in (
                image_feats, cam_weights, depth_weight.T, ray_bins, pillar_sums,
                pillar_counts.T, lidar_weight, out_cotangent,
            )
        ],
    )
    _, feat, share, lifted, note, far, probs, gain, merge_held = front(
        me, padded, across, beside, held, depth_pad, spread, masks, side,
        pinned(cam_weights), pinned(merge_weight),
    )
    partner = swapped(note, -1)
    far_got = swapped(jnp.concatenate([far, note[0:6]], 0), 3)[0:2]
    wide = lambda a: a.astype(F32)
    four = jnp.zeros((4, BR, C), F32)
    mine = lifted.reshape(WIN, BR, C)
    rise = mine[2:12] + jnp.concatenate([four, wide(partner[2:8])], 0)
    fall = mine[4:14] + jnp.concatenate([wide(partner[8:14]), four], 0)
    crossing = jnp.concatenate(
        [
            jnp.where(odd, fall, rise).astype(BF16),
            note[16:20],
            jnp.where(odd, partner[19:20], partner[16:17]),
            note[20:22],
            jnp.where(odd, partner[21:22], partner[20:21]),
        ],
        axis=0,
    )
    crossed = swapped(crossing, 1)
    relay = jnp.concatenate(
        [
            jnp.where(odd, crossed[0:6], crossed[4:10]),
            jnp.where(odd, crossed[10:11], crossed[13:14]),
            jnp.where(odd, crossed[15:16], crossed[16:17]),
        ],
        axis=0,
    )
    relayed = swapped(relay, -1)
    merged, cam_grad, lid_grad = back(
        me, lifted, note, partner, crossed, relayed, far_got, merge_held, feat, share,
        probs, gain, slots, depth_pad, spread,
    )
    return merged, cam_grad, lid_grad.reshape(BR, BA, CL)


def solution(mesh):
    columns = P(None, AXES, None)
    placed = (
        columns, P(), P(), P(AXES, None), columns, P(None, AXES), P(), P(), columns,
    )
    return jax.shard_map(
        local, mesh=mesh, in_specs=placed, out_specs=(columns,) * 3, check_vma=False
    )
```

```python
import jax
import jax.numpy as jnp
from jax import lax
from jax.experimental import pallas as pl
from jax.experimental.pallas import tpu as pltpu
from jax.sharding import PartitionSpec as P

AXES = ("branch", "strip")
ROWS = 32
COLS = 64
WIDE = 72
HALO = (WIDE - COLS) // 2
C = 256
CL = 128
BINS = 118
LANES = 128
LAYERS = 3
BR = 16
BA = 4
WIN = 16
REACH = 6
SLOTS = 12
BLOCK = 16
TILE_H = 16
TILE = TILE_H * COLS
UNROLL = 2
TALL_H = 16
TALL = TALL_H * COLS
F32 = jnp.float32
BF16 = jnp.bfloat16


def whole(memory_space=pltpu.VMEM):
    return pl.BlockSpec(memory_space=memory_space)


def iota(shape, dim):
    return lax.broadcasted_iota(jnp.int32, shape, dim)


def nt_dot(lhs, rhs):
    return lax.dot_general(lhs, rhs, (((1,), (1,)), ((), ())), preferred_element_type=F32)


def tn_dot(lhs, rhs):
    return lax.dot_general(lhs, rhs, (((0,), (0,)), ((), ())), preferred_element_type=F32)


def dot(lhs, rhs):
    return jnp.dot(lhs, rhs, preferred_element_type=F32)


def fill_spread(spread):
    bin_index = iota((LANES, WIN * BR), 0)
    column = iota((LANES, WIN * BR), 1)
    for slot in range(SLOTS):
        offset = (column - (slot + 2) * BR) * BINS
        hit = (offset <= bin_index * BR) & (bin_index * BR < offset + BINS)
        spread[slot * LANES : (slot + 1) * LANES, :] = hit.astype(F32).astype(BF16)


def fill_side(side, pillars, counts, lidar, cotangent, flat):
    for cycle in range(BR):
        flat[BA * cycle : BA * (cycle + 1), :] = cotangent[cycle].astype(F32)
    order = iota((BA * BR, BR * BA), 0)
    source = iota((BA * BR, BR * BA), 1)
    swap = ((order % BR) * BA + order // BR == source).astype(F32).astype(BF16)
    side[0:BA] = dot(swap, flat[...].astype(BF16)).astype(BF16).reshape(BA, BR, C)
    cells = 4 * BR * BA
    row = iota((cells, 2 * BR), 0)
    pick = (row // (2 * BA) == iota((cells, 2 * BR), 1)).astype(F32).astype(BF16)
    spread = nt_dot(pick, counts[...].astype(F32).astype(BF16))
    here = iota((cells, 2 * BA), 0) % (2 * BA) == iota((cells, 2 * BA), 1)
    count = jnp.sum(jnp.where(here, spread, 0.0), axis=1, keepdims=True)
    scale = jnp.where(count > 0.0, 1.0, 0.0) / jnp.maximum(count, 1.0)
    feats = (pillars[...].astype(F32).reshape(cells, CL) * scale).astype(BF16)
    goal = iota((BA * BR, cells), 0)
    origin = iota((BA * BR, cells), 1)
    base = (goal % BR) * (4 * BA) + (goal // BR) * 2
    total = None
    for offset in range(4):
        step = (offset // 2) * 2 * BA + offset % 2
        chosen = dot((base + step == origin).astype(F32).astype(BF16), feats).astype(BF16)
        part = dot(chosen, lidar[offset])
        total = part if total is None else total + part
    lid = jnp.maximum(total, 0.0).astype(BF16)
    for pair in range(2):
        top = pair * 2 * BR
        side[BA + pair] = jnp.concatenate(
            [lid[top : top + BR], lid[top + BR : top + 2 * BR]], axis=1
        )


def prepare_kernel(
    me_ref, image, weights, depth_hbm, bins_hbm, pillars_hbm, counts_hbm, lidar_hbm,
    cotangent_hbm,
    padded, held, spread, depth_pad, masks, slot_out, side,
    depth, bins, pillars, counts, lidar, cotangent, flat, sems,
):
    copies = [
        pltpu.make_async_copy(source, target, sems.at[index])
        for index, (source, target) in enumerate(
            [
                (depth_hbm, depth),
                (bins_hbm, bins),
                (pillars_hbm, pillars),
                (counts_hbm, counts),
                (lidar_hbm, lidar),
                (cotangent_hbm, cotangent),
                (image, padded.at[pl.ds(1, ROWS), pl.ds(0, COLS)]),
                (weights.at[0], held),
            ]
        )
    ]
    for copy in copies:
        copy.start()
    padded[0] = jnp.zeros((WIDE, C), BF16)
    padded[ROWS + 1] = jnp.zeros((WIDE, C), BF16)
    fill_spread(spread)
    for copy in copies[:6]:
        copy.wait()
    depth_pad[BINS - 6 :, :] = jnp.zeros((LANES - BINS + 6, C), BF16)
    depth_pad[0:BINS, :] = depth[...]
    fill_side(side, pillars, counts, lidar, cotangent, flat)
    cells = bins[...]
    sector = cells // (BR * BA)
    step = sector - me_ref[0] + 1
    step = jnp.where(step < 0, step + 256, step)
    step = jnp.where(step > 255, step - 256, step)
    slot_out[...] = jnp.full((COLS, LANES), -1, jnp.int32)
    slot_out[:, 0:BINS] = step * BA + cells % BA
    slot_map = slot_out[...]
    for index in range(SLOTS):
        masks[index] = (slot_map == index).astype(F32).astype(BF16)
    for copy in copies[6:]:
        copy.wait()


def prepare(*operands):
    return pl.pallas_call(
        prepare_kernel,
        out_shape=(
            jax.ShapeDtypeStruct((ROWS + 2, WIDE, C), BF16),
            jax.ShapeDtypeStruct((9, C, C), BF16),
            jax.ShapeDtypeStruct((SLOTS * LANES, WIN * BR), BF16),
            jax.ShapeDtypeStruct((LANES, C), BF16),
            jax.ShapeDtypeStruct((SLOTS, COLS, LANES), BF16),
            jax.ShapeDtypeStruct((COLS, LANES), jnp.int32),
            jax.ShapeDtypeStruct((6, BR, C), BF16),
        ),
        in_specs=[whole(pltpu.SMEM)] + [whole(pltpu.HBM)] * 8,
        out_specs=(whole(),) * 7,
        scratch_shapes=[
            pltpu.VMEM((BINS, C), BF16),
            pltpu.VMEM((COLS, BINS), jnp.int32),
            pltpu.VMEM((2 * BR, 2 * BA, CL), BF16),
            pltpu.VMEM((2 * BA, 2 * BR), jnp.int32),
            pltpu.VMEM((4, CL, CL), BF16),
            pltpu.VMEM((BR, BA, C), BF16),
            pltpu.VMEM((BR * BA, C), F32),
            pltpu.SemaphoreType.DMA((8,)),
        ],
        compiler_params=pltpu.CompilerParams(vmem_limit_bytes=24 * 2**20),
        cost_estimate=pl.CostEstimate(flops=10**8, bytes_accessed=8 * 2**20, transcendentals=0),
        name="prepare",
    )(*operands)


def front_kernel(
    me_ref, padded_in, crossed, beside, held_first, depth_pad, spread, masks, side,
    weights, merging,
    first, feat_out, share_out, lifted_out, note_out, far_out, probs_out, gain_out, merge_held,
    second, held_rest, sems,
):
    copies = [
        pltpu.make_async_copy(weights.at[1], held_rest.at[0], sems.at[0]),
        pltpu.make_async_copy(weights.at[2], held_rest.at[1], sems.at[1]),
        pltpu.make_async_copy(merging, merge_held, sems.at[2]),
    ]
    for copy in copies:
        copy.start()
    odd = lax.rem(me_ref[0], 2)
    second[0] = jnp.zeros((WIDE, C), BF16)
    second[ROWS + 1] = jnp.zeros((WIDE, C), BF16)

    def put_halo(right, left):
        first[1 : ROWS + 1, COLS:WIDE, :] = jnp.concatenate(
            [right[...].astype(F32), left[...].astype(F32)], axis=1
        ).astype(BF16)

    @pl.when(odd == 1)
    def _():
        put_halo(crossed, beside)

    @pl.when(odd == 0)
    def _():
        put_halo(beside, crossed)

    note_out[WIN : WIN + 6] = side[...]

    def convolved(source, held, top, narrow):
        lhs = jnp.concatenate(
            [
                source[pl.ds(top + down, BLOCK)].reshape(BLOCK * WIDE, C)
                for down in range(3)
            ],
            axis=1,
        )
        out = None
        for right in (1, 0, 2):
            kernel = jnp.concatenate(
                [held[3 * down + right] for down in range(3)], axis=0
            )
            if narrow and right == 1:
                part = dot(
                    lhs.reshape(BLOCK, WIDE, 3 * C)[:, 0:COLS].reshape(BLOCK * COLS, 3 * C),
                    kernel,
                ).reshape(BLOCK, COLS, C)
            else:
                part = dot(lhs, kernel).reshape(BLOCK, WIDE, C)
                if right != 1:
                    part = pltpu.roll(part, (1 - right) % WIDE, 1)
                if narrow:
                    part = part[:, 0:COLS]
            out = part if out is None else out + part
        return jnp.maximum(out, 0.0).astype(BF16)

    for index, (source, target) in enumerate([(first, second), (second, first)]):
        if index == 1:
            copies[0].wait()
        held = held_first if index == 0 else held_rest.at[0]
        for block in range(ROWS // BLOCK):
            target[block * BLOCK + 1 : (block + 1) * BLOCK + 1] = convolved(
                source, held, block * BLOCK, False
            )
    copies[1].wait()
    for block in range(ROWS // BLOCK):
        feat_out[block * BLOCK * COLS : (block + 1) * BLOCK * COLS, :] = convolved(
            first, held_rest.at[1], block * BLOCK, True
        ).reshape(BLOCK * COLS, C)

    lane_ok = iota((TILE, LANES), 1) < BINS

    @pl.loop(0, ROWS // TILE_H, unroll=UNROLL)
    def _(tile):
        rows = pl.ds(pl.multiple_of(tile * TILE, TILE), TILE)
        logits = nt_dot(feat_out[rows, :], depth_pad[...])
        decay = jnp.exp(-jnp.abs(logits))
        tail = jnp.log(1.0 + decay)
        soft = jnp.maximum(logits, 0.0) + tail + 0.05
        soft = jnp.where(lane_ok, soft, 0.0)
        scale = 1.0 / jnp.sum(soft, axis=1, keepdims=True)
        probs = soft * scale
        gate = jnp.exp(jnp.minimum(logits, 0.0) - tail)
        probs_out[rows, :] = probs
        gain_out[rows, :] = gate * scale
        low = probs.astype(BF16).reshape(TILE_H, COLS, LANES)
        share_out[rows, :] = dot(
            jnp.concatenate(
                [
                    (low * masks[index][None]).reshape(TILE, LANES)
                    for index in range(SLOTS)
                ],
                axis=1,
            ),
            spread[...],
        ).astype(BF16)

    lifted = tn_dot(share_out[...], feat_out[...])
    lifted_out[...] = lifted
    note_out[0:WIN] = lifted.astype(BF16).reshape(WIN, BR, C)
    copies[2].wait()

    @pl.when(odd == 1)
    def _():
        far_out[...] = note_out[12:14]

    @pl.when(odd == 0)
    def _():
        far_out[...] = note_out[2:4]


def front(*operands):
    total = ROWS * COLS
    return pl.pallas_call(
        front_kernel,
        out_shape=(
            jax.ShapeDtypeStruct((ROWS + 2, WIDE, C), BF16),
            jax.ShapeDtypeStruct((total, C), BF16),
            jax.ShapeDtypeStruct((total, WIN * BR), BF16),
            jax.ShapeDtypeStruct((WIN * BR, C), F32),
            jax.ShapeDtypeStruct((WIN + 6, BR, C), BF16),
            jax.ShapeDtypeStruct((2, BR, C), BF16),
            jax.ShapeDtypeStruct((total, LANES), F32),
            jax.ShapeDtypeStruct((total, LANES), F32),
            jax.ShapeDtypeStruct((9, C + CL, C), BF16),
        ),
        in_specs=[whole(pltpu.SMEM)] + [whole()] * 8 + [whole(pltpu.HBM)] * 2,
        out_specs=(whole(),) * 9,
        scratch_shapes=[
            pltpu.VMEM((ROWS + 2, WIDE, C), BF16),
            pltpu.VMEM((LAYERS - 1, 9, C, C), BF16),
            pltpu.SemaphoreType.DMA((3,)),
        ],
        input_output_aliases={1: 0},
        compiler_params=pltpu.CompilerParams(vmem_limit_bytes=32 * 2**20),
        name="front",
    )(*operands)


def along_cycles(part, down):
    if down == 0:
        return part
    cycle = iota(part.shape, 1)
    moved = pltpu.roll(part, down % BR, 1)
    keep = cycle >= 1 if down == 1 else cycle < BR - 1
    return jnp.where(keep, moved, 0.0)


def back_kernel(
    me_ref, lifted, note, partner, crossed, relayed, far, weights, feat, share, probs, gain,
    slots, depth_pad, spread,
    merged_out, cam_out, lid_out,
    cam, cot, lid, table, wide_table,
):

    def put_lid(at, packed):
        lid[at] = packed[:, 0:CL]
        lid[at + 1] = packed[:, CL:]

    cam[...] = lifted[...].reshape(WIN, BR, C)
    cot[REACH : REACH + BA] = note[WIN : WIN + BA]
    put_lid(REACH, note[WIN + BA])
    put_lid(REACH + 2, note[WIN + BA + 1])
    cot[0] = jnp.zeros((BR, C), BF16)
    cot[WIN - 1] = jnp.zeros((BR, C), BF16)
    odd = lax.rem(me_ref[0], 2)

    def gather(low_side):
        near = 10 if low_side else 2
        other = 2 if low_side else 10
        cam[6:16] += (partner[2:12] if low_side else crossed[0:10]).astype(F32)
        cam[0:10] += (crossed[0:10] if low_side else partner[4:14]).astype(F32)
        start = 10 if low_side else 0
        cam[start : start + 6] += relayed[0:6].astype(F32)
        edge = 0 if low_side else 14
        cam[edge : edge + 2] += far[...].astype(F32)
        cot[near : near + 4] = partner[WIN : WIN + 4]
        cot[other : other + 4] = crossed[10:14]
        cot[1 if low_side else 14] = crossed[14]
        cot[14 if low_side else 1] = relayed[6]
        put_lid(near, partner[WIN + 4])
        put_lid(near + 2, partner[WIN + 5])
        put_lid(other, crossed[15])
        put_lid(other + 2, crossed[16])
        put_lid(0 if low_side else 14, crossed[17])
        put_lid(14 if low_side else 0, relayed[7])

    @pl.when(odd == 0)
    def _():
        gather(True)

    @pl.when(odd == 1)
    def _():
        gather(False)

    span = WIN - 2
    merged_in = jnp.concatenate([cam[...].astype(BF16), lid[...]], axis=2)
    joined = jnp.concatenate(
        [merged_in[right : right + span].reshape(span * BR, C + CL) for right in range(3)],
        axis=1,
    )
    pre = None
    for down in range(3):
        kernel = jnp.concatenate([weights[3 * down + right] for right in range(3)], axis=0)
        part = along_cycles(dot(joined, kernel).reshape(span, BR, C), 1 - down)
        pre = part if pre is None else pre + part
    gate = 1.0 / (1.0 + jnp.exp(-pre))
    merged = (pre * gate).astype(BF16)
    grad_pre = (
        cot[1 : WIN - 1].astype(F32) * (gate * (1.0 + pre * (1.0 - gate)))
    ).astype(BF16)
    inner = span - 2
    total = None
    for down in range(3):
        part = None
        for right in range(3):
            piece = nt_dot(
                grad_pre[2 - right : 2 - right + inner].reshape(inner * BR, C),
                weights[3 * down + right],
            )
            part = piece if part is None else part + piece
        part = along_cycles(part.reshape(inner, BR, C + CL), down - 1)
        total = part if total is None else total + part
    table[0 : 2 * BR, :] = jnp.zeros((2 * BR, C), BF16)
    table[(WIN - 2) * BR :, :] = jnp.zeros((2 * BR, C), BF16)
    table[2 * BR : (WIN - 2) * BR, :] = total[:, :, 0:C].astype(BF16).reshape(inner * BR, C)
    order = iota((BR * BA, BR * BA), 0)
    source = iota((BR * BA, BR * BA), 1)
    swap = ((order % BA) * BR + order // BA == source).astype(F32).astype(BF16)
    own = merged[REACH - 1 : REACH - 1 + BA].reshape(BA * BR, C)
    turned = dot(swap, own)
    for cycle in range(BR):
        merged_out[cycle] = turned[BA * cycle : BA * (cycle + 1)].astype(BF16)
    own_lid = total[REACH - 2 : REACH - 2 + BA, :, C:].astype(BF16).reshape(BA * BR, CL)
    lid_out[...] = dot(swap, own_lid).astype(BF16)
    wide_table[...] = dot(spread[...], table[...]).astype(BF16)

    @pl.loop(0, ROWS // TALL_H, unroll=True)
    def _(tile):
        rows = pl.ds(pl.multiple_of(tile * TALL, TALL), TALL)
        block = feat[rows, :]
        slot_map = slots[...]
        picked = jnp.zeros((TALL_H, COLS, LANES), F32)
        for pair in range(SLOTS // 2):
            both = nt_dot(block, wide_table[pair * 2 * LANES : (pair + 1) * 2 * LANES, :])
            for side in range(2):
                value = both[:, side * LANES : (side + 1) * LANES].reshape(
                    TALL_H, COLS, LANES
                )
                picked = jnp.where((slot_map == 2 * pair + side)[None], value, picked)
        picked = picked.reshape(TALL, LANES)
        mean = jnp.sum(picked * probs[rows, :], axis=1, keepdims=True)
        grad_logits = ((picked - mean) * gain[rows, :]).astype(BF16)
        out = dot(share[rows, :], table[...]) + dot(grad_logits, depth_pad[...])
        cam_out[pl.ds(tile * TALL_H, TALL_H)] = out.astype(BF16).reshape(TALL_H, COLS, C)


def back(*operands):
    return pl.pallas_call(
        back_kernel,
        out_shape=(
            jax.ShapeDtypeStruct((BR, BA, C), BF16),
            jax.ShapeDtypeStruct((ROWS, COLS, C), BF16),
            jax.ShapeDtypeStruct((BR * BA, CL), BF16),
        ),
        in_specs=[whole(pltpu.SMEM)] + [whole()] * 14,
        out_specs=(whole(),) * 3,
        scratch_shapes=[
            pltpu.VMEM((WIN, BR, C), F32),
            pltpu.VMEM((WIN, BR, C), BF16),
            pltpu.VMEM((WIN, BR, CL), BF16),
            pltpu.VMEM((WIN * BR, C), BF16),
            pltpu.VMEM((SLOTS * LANES, C), BF16),
        ],
        compiler_params=pltpu.CompilerParams(vmem_limit_bytes=32 * 2**20),
        name="back",
    )(*operands)


def swapped(block, odd_step):
    count = lax.axis_size(AXES)
    route = [(i, (i + odd_step if i % 2 else i - odd_step) % count) for i in range(count)]
    return lax.ppermute(block, AXES, route)


def local(
    image_feats, cam_weights, depth_weight, ray_bins, pillar_sums, pillar_counts,
    lidar_weight, merge_weight, out_cotangent,
):
    me = lax.axis_index(AXES).astype(jnp.int32)
    odd = me % 2 == 1
    me = me.reshape(1)
    left_edge = image_feats[:, 0:HALO]
    right_edge = image_feats[:, COLS - HALO :]
    beside = swapped(jnp.where(odd, left_edge, right_edge), -1)
    across = swapped(jnp.where(odd, right_edge, left_edge), 1)
    pinned = lambda value: pltpu.with_memory_space_constraint(value, pltpu.HBM)
    padded, held, spread, depth_pad, masks, slots, side = prepare(
        me,
        *[
            pinned(value)
            for value in (
                image_feats, cam_weights, depth_weight.T, ray_bins, pillar_sums,
                pillar_counts.T, lidar_weight, out_cotangent,
            )
        ],
    )
    _, feat, share, lifted, note, far, probs, gain, merge_held = front(
        me, padded, across, beside, held, depth_pad, spread, masks, side,
        pinned(cam_weights), pinned(merge_weight),
    )
    partner = swapped(note, -1)
    far_got = swapped(jnp.concatenate([far, note[0:6]], 0), 3)[0:2]
    wide = lambda a: a.astype(F32)
    four = jnp.zeros((4, BR, C), F32)
    mine = lifted.reshape(WIN, BR, C)
    rise = mine[2:12] + jnp.concatenate([four, wide(partner[2:8])], 0)
    fall = mine[4:14] + jnp.concatenate([wide(partner[8:14]), four], 0)
    crossing = jnp.concatenate(
        [
            jnp.where(odd, fall, rise).astype(BF16),
            note[16:20],
            jnp.where(odd, partner[19:20], partner[16:17]),
            note[20:22],
            jnp.where(odd, partner[21:22], partner[20:21]),
        ],
        axis=0,
    )
    crossed = swapped(crossing, 1)
    relay = jnp.concatenate(
        [
            jnp.where(odd, crossed[0:6], crossed[4:10]),
            jnp.where(odd, crossed[10:11], crossed[13:14]),
            jnp.where(odd, crossed[15:16], crossed[16:17]),
        ],
        axis=0,
    )
    relayed = swapped(relay, -1)
    merged, cam_grad, lid_grad = back(
        me, lifted, note, partner, crossed, relayed, far_got, merge_held, feat, share,
        probs, gain, slots, depth_pad, spread,
    )
    return merged, cam_grad, lid_grad.reshape(BR, BA, CL)


def solution(mesh):
    columns = P(None, AXES, None)
    placed = (
        columns, P(), P(), P(AXES, None), columns, P(None, AXES), P(), P(), columns,
    )
    return jax.shard_map(
        local, mesh=mesh, in_specs=placed, out_specs=(columns,) * 3, check_vma=False
    )
```

```python
import jax
import jax.numpy as jnp
from jax import lax
from jax.experimental import pallas as pl
from jax.experimental.pallas import tpu as pltpu
from jax.sharding import PartitionSpec as P

AXES = ("branch", "strip")
ROWS = 32
COLS = 64
WIDE = 72
HALO = (WIDE - COLS) // 2
C = 256
CL = 128
BINS = 118
LANES = 128
LAYERS = 3
BR = 16
BA = 4
WIN = 16
REACH = 6
SLOTS = 12
BLOCK = 16
TILE_H = 16
TILE = TILE_H * COLS
UNROLL = 2
TALL_H = 8
TALL = TALL_H * COLS
F32 = jnp.float32
BF16 = jnp.bfloat16


def whole(memory_space=pltpu.VMEM):
    return pl.BlockSpec(memory_space=memory_space)


def iota(shape, dim):
    return lax.broadcasted_iota(jnp.int32, shape, dim)


def nt_dot(lhs, rhs):
    return lax.dot_general(lhs, rhs, (((1,), (1,)), ((), ())), preferred_element_type=F32)


def tn_dot(lhs, rhs):
    return lax.dot_general(lhs, rhs, (((0,), (0,)), ((), ())), preferred_element_type=F32)


def dot(lhs, rhs):
    return jnp.dot(lhs, rhs, preferred_element_type=F32)


def fill_spread(spread):
    bin_index = iota((LANES, WIN * BR), 0)
    column = iota((LANES, WIN * BR), 1)
    for slot in range(SLOTS):
        offset = (column - (slot + 2) * BR) * BINS
        hit = (offset <= bin_index * BR) & (bin_index * BR < offset + BINS)
        spread[slot * LANES : (slot + 1) * LANES, :] = hit.astype(F32).astype(BF16)


def fill_side(side, pillars, counts, lidar, cotangent, flat):
    for cycle in range(BR):
        flat[BA * cycle : BA * (cycle + 1), :] = cotangent[cycle].astype(F32)
    order = iota((BA * BR, BR * BA), 0)
    source = iota((BA * BR, BR * BA), 1)
    swap = ((order % BR) * BA + order // BR == source).astype(F32).astype(BF16)
    side[0:BA] = dot(swap, flat[...].astype(BF16)).astype(BF16).reshape(BA, BR, C)
    cells = 4 * BR * BA
    row = iota((cells, 2 * BR), 0)
    pick = (row // (2 * BA) == iota((cells, 2 * BR), 1)).astype(F32).astype(BF16)
    spread = nt_dot(pick, counts[...].astype(F32).astype(BF16))
    here = iota((cells, 2 * BA), 0) % (2 * BA) == iota((cells, 2 * BA), 1)
    count = jnp.sum(jnp.where(here, spread, 0.0), axis=1, keepdims=True)
    scale = jnp.where(count > 0.0, 1.0, 0.0) / jnp.maximum(count, 1.0)
    feats = (pillars[...].astype(F32).reshape(cells, CL) * scale).astype(BF16)
    goal = iota((BA * BR, cells), 0)
    origin = iota((BA * BR, cells), 1)
    base = (goal % BR) * (4 * BA) + (goal // BR) * 2
    total = None
    for offset in range(4):
        step = (offset // 2) * 2 * BA + offset % 2
        chosen = dot((base + step == origin).astype(F32).astype(BF16), feats).astype(BF16)
        part = dot(chosen, lidar[offset])
        total = part if total is None else total + part
    lid = jnp.maximum(total, 0.0).astype(BF16)
    for pair in range(2):
        top = pair * 2 * BR
        side[BA + pair] = jnp.concatenate(
            [lid[top : top + BR], lid[top + BR : top + 2 * BR]], axis=1
        )


def prepare_kernel(
    me_ref, image, weights, depth_hbm, bins_hbm, pillars_hbm, counts_hbm, lidar_hbm,
    cotangent_hbm,
    padded, held, spread, depth_pad, masks, slot_out, side,
    depth, bins, pillars, counts, lidar, cotangent, flat, sems,
):
    copies = [
        pltpu.make_async_copy(source, target, sems.at[index])
        for index, (source, target) in enumerate(
            [
                (depth_hbm, depth),
                (bins_hbm, bins),
                (pillars_hbm, pillars),
                (counts_hbm, counts),
                (lidar_hbm, lidar),
                (cotangent_hbm, cotangent),
                (image, padded.at[pl.ds(1, ROWS), pl.ds(0, COLS)]),
                (weights.at[0], held),
            ]
        )
    ]
    for copy in copies:
        copy.start()
    padded[0] = jnp.zeros((WIDE, C), BF16)
    padded[ROWS + 1] = jnp.zeros((WIDE, C), BF16)
    fill_spread(spread)
    for copy in copies[:6]:
        copy.wait()
    depth_pad[BINS - 6 :, :] = jnp.zeros((LANES - BINS + 6, C), BF16)
    depth_pad[0:BINS, :] = depth[...]
    fill_side(side, pillars, counts, lidar, cotangent, flat)
    cells = bins[...]
    sector = cells // (BR * BA)
    step = sector - me_ref[0] + 1
    step = jnp.where(step < 0, step + 256, step)
    step = jnp.where(step > 255, step - 256, step)
    slot_out[...] = jnp.full((COLS, LANES), -1, jnp.int32)
    slot_out[:, 0:BINS] = step * BA + cells % BA
    slot_map = slot_out[...]
    for index in range(SLOTS):
        masks[index] = (slot_map == index).astype(F32).astype(BF16)
    for copy in copies[6:]:
        copy.wait()


def prepare(*operands):
    return pl.pallas_call(
        prepare_kernel,
        out_shape=(
            jax.ShapeDtypeStruct((ROWS + 2, WIDE, C), BF16),
            jax.ShapeDtypeStruct((9, C, C), BF16),
            jax.ShapeDtypeStruct((SLOTS * LANES, WIN * BR), BF16),
            jax.ShapeDtypeStruct((LANES, C), BF16),
            jax.ShapeDtypeStruct((SLOTS, COLS, LANES), BF16),
            jax.ShapeDtypeStruct((COLS, LANES), jnp.int32),
            jax.ShapeDtypeStruct((6, BR, C), BF16),
        ),
        in_specs=[whole(pltpu.SMEM)] + [whole(pltpu.HBM)] * 8,
        out_specs=(whole(),) * 7,
        scratch_shapes=[
            pltpu.VMEM((BINS, C), BF16),
            pltpu.VMEM((COLS, BINS), jnp.int32),
            pltpu.VMEM((2 * BR, 2 * BA, CL), BF16),
            pltpu.VMEM((2 * BA, 2 * BR), jnp.int32),
            pltpu.VMEM((4, CL, CL), BF16),
            pltpu.VMEM((BR, BA, C), BF16),
            pltpu.VMEM((BR * BA, C), F32),
            pltpu.SemaphoreType.DMA((8,)),
        ],
        compiler_params=pltpu.CompilerParams(vmem_limit_bytes=24 * 2**20),
        cost_estimate=pl.CostEstimate(flops=10**8, bytes_accessed=8 * 2**20, transcendentals=0),
        name="prepare",
    )(*operands)


def front_kernel(
    me_ref, padded_in, crossed, beside, held_first, depth_pad, spread, masks, side,
    weights, merging,
    first, feat_out, share_out, lifted_out, note_out, far_out, probs_out, gain_out, merge_held,
    second, held_rest, sems,
):
    copies = [
        pltpu.make_async_copy(weights.at[1], held_rest.at[0], sems.at[0]),
        pltpu.make_async_copy(weights.at[2], held_rest.at[1], sems.at[1]),
        pltpu.make_async_copy(merging, merge_held, sems.at[2]),
    ]
    for copy in copies:
        copy.start()
    odd = lax.rem(me_ref[0], 2)
    second[0] = jnp.zeros((WIDE, C), BF16)
    second[ROWS + 1] = jnp.zeros((WIDE, C), BF16)

    def put_halo(right, left):
        first[1 : ROWS + 1, COLS:WIDE, :] = jnp.concatenate(
            [right[...].astype(F32), left[...].astype(F32)], axis=1
        ).astype(BF16)

    @pl.when(odd == 1)
    def _():
        put_halo(crossed, beside)

    @pl.when(odd == 0)
    def _():
        put_halo(beside, crossed)

    note_out[WIN : WIN + 6] = side[...]

    def convolved(source, held, top, narrow):
        lhs = jnp.concatenate(
            [
                source[pl.ds(top + down, BLOCK)].reshape(BLOCK * WIDE, C)
                for down in range(3)
            ],
            axis=1,
        )
        out = None
        for right in (1, 0, 2):
            kernel = jnp.concatenate(
                [held[3 * down + right] for down in range(3)], axis=0
            )
            if narrow and right == 1:
                part = dot(
                    lhs.reshape(BLOCK, WIDE, 3 * C)[:, 0:COLS].reshape(BLOCK * COLS, 3 * C),
                    kernel,
                ).reshape(BLOCK, COLS, C)
            else:
                part = dot(lhs, kernel).reshape(BLOCK, WIDE, C)
                if right != 1:
                    part = pltpu.roll(part, (1 - right) % WIDE, 1)
                if narrow:
                    part = part[:, 0:COLS]
            out = part if out is None else out + part
        return jnp.maximum(out, 0.0).astype(BF16)

    for index, (source, target) in enumerate([(first, second), (second, first)]):
        if index == 1:
            copies[0].wait()
        held = held_first if index == 0 else held_rest.at[0]
        for block in range(ROWS // BLOCK):
            target[block * BLOCK + 1 : (block + 1) * BLOCK + 1] = convolved(
                source, held, block * BLOCK, False
            )
    copies[1].wait()
    for block in range(ROWS // BLOCK):
        feat_out[block * BLOCK * COLS : (block + 1) * BLOCK * COLS, :] = convolved(
            first, held_rest.at[1], block * BLOCK, True
        ).reshape(BLOCK * COLS, C)

    lane_ok = iota((TILE, LANES), 1) < BINS

    @pl.loop(0, ROWS // TILE_H, unroll=UNROLL)
    def _(tile):
        rows = pl.ds(pl.multiple_of(tile * TILE, TILE), TILE)
        logits = nt_dot(feat_out[rows, :], depth_pad[...])
        decay = jnp.exp(-jnp.abs(logits))
        tail = jnp.log(1.0 + decay)
        soft = jnp.maximum(logits, 0.0) + tail + 0.05
        soft = jnp.where(lane_ok, soft, 0.0)
        scale = 1.0 / jnp.sum(soft, axis=1, keepdims=True)
        probs = soft * scale
        gate = jnp.exp(jnp.minimum(logits, 0.0) - tail)
        probs_out[rows, :] = probs
        gain_out[rows, :] = gate * scale
        low = probs.astype(BF16).reshape(TILE_H, COLS, LANES)
        share_out[rows, :] = dot(
            jnp.concatenate(
                [
                    (low * masks[index][None]).reshape(TILE, LANES)
                    for index in range(SLOTS)
                ],
                axis=1,
            ),
            spread[...],
        ).astype(BF16)

    lifted = tn_dot(share_out[...], feat_out[...])
    lifted_out[...] = lifted
    note_out[0:WIN] = lifted.astype(BF16).reshape(WIN, BR, C)
    copies[2].wait()

    @pl.when(odd == 1)
    def _():
        far_out[...] = note_out[12:14]

    @pl.when(odd == 0)
    def _():
        far_out[...] = note_out[2:4]


def front(*operands):
    total = ROWS * COLS
    return pl.pallas_call(
        front_kernel,
        out_shape=(
            jax.ShapeDtypeStruct((ROWS + 2, WIDE, C), BF16),
            jax.ShapeDtypeStruct((total, C), BF16),
            jax.ShapeDtypeStruct((total, WIN * BR), BF16),
            jax.ShapeDtypeStruct((WIN * BR, C), F32),
            jax.ShapeDtypeStruct((WIN + 6, BR, C), BF16),
            jax.ShapeDtypeStruct((2, BR, C), BF16),
            jax.ShapeDtypeStruct((total, LANES), F32),
            jax.ShapeDtypeStruct((total, LANES), F32),
            jax.ShapeDtypeStruct((9, C + CL, C), BF16),
        ),
        in_specs=[whole(pltpu.SMEM)] + [whole()] * 8 + [whole(pltpu.HBM)] * 2,
        out_specs=(whole(),) * 9,
        scratch_shapes=[
            pltpu.VMEM((ROWS + 2, WIDE, C), BF16),
            pltpu.VMEM((LAYERS - 1, 9, C, C), BF16),
            pltpu.SemaphoreType.DMA((3,)),
        ],
        input_output_aliases={1: 0},
        compiler_params=pltpu.CompilerParams(vmem_limit_bytes=32 * 2**20),
        name="front",
    )(*operands)


def along_cycles(part, down):
    if down == 0:
        return part
    cycle = iota(part.shape, 1)
    moved = pltpu.roll(part, down % BR, 1)
    keep = cycle >= 1 if down == 1 else cycle < BR - 1
    return jnp.where(keep, moved, 0.0)


def back_kernel(
    me_ref, lifted, note, partner, crossed, relayed, far, weights, feat, share, probs, gain,
    slots, depth_pad, spread,
    merged_out, cam_out, lid_out,
    cam, cot, lid, table, wide_table,
):

    def put_lid(at, packed):
        lid[at] = packed[:, 0:CL]
        lid[at + 1] = packed[:, CL:]

    cam[...] = lifted[...].reshape(WIN, BR, C)
    cot[REACH : REACH + BA] = note[WIN : WIN + BA]
    put_lid(REACH, note[WIN + BA])
    put_lid(REACH + 2, note[WIN + BA + 1])
    cot[0] = jnp.zeros((BR, C), BF16)
    cot[WIN - 1] = jnp.zeros((BR, C), BF16)
    odd = lax.rem(me_ref[0], 2)

    def gather(low_side):
        near = 10 if low_side else 2
        other = 2 if low_side else 10
        cam[6:16] += (partner[2:12] if low_side else crossed[0:10]).astype(F32)
        cam[0:10] += (crossed[0:10] if low_side else partner[4:14]).astype(F32)
        start = 10 if low_side else 0
        cam[start : start + 6] += relayed[0:6].astype(F32)
        edge = 0 if low_side else 14
        cam[edge : edge + 2] += far[...].astype(F32)
        cot[near : near + 4] = partner[WIN : WIN + 4]
        cot[other : other + 4] = crossed[10:14]
        cot[1 if low_side else 14] = crossed[14]
        cot[14 if low_side else 1] = relayed[6]
        put_lid(near, partner[WIN + 4])
        put_lid(near + 2, partner[WIN + 5])
        put_lid(other, crossed[15])
        put_lid(other + 2, crossed[16])
        put_lid(0 if low_side else 14, crossed[17])
        put_lid(14 if low_side else 0, relayed[7])

    @pl.when(odd == 0)
    def _():
        gather(True)

    @pl.when(odd == 1)
    def _():
        gather(False)

    span = WIN - 2
    merged_in = jnp.concatenate([cam[...].astype(BF16), lid[...]], axis=2)
    joined = jnp.concatenate(
        [merged_in[right : right + span].reshape(span * BR, C + CL) for right in range(3)],
        axis=1,
    )
    pre = None
    for down in range(3):
        kernel = jnp.concatenate([weights[3 * down + right] for right in range(3)], axis=0)
        part = along_cycles(dot(joined, kernel).reshape(span, BR, C), 1 - down)
        pre = part if pre is None else pre + part
    gate = 1.0 / (1.0 + jnp.exp(-pre))
    merged = (pre * gate).astype(BF16)
    grad_pre = (
        cot[1 : WIN - 1].astype(F32) * (gate * (1.0 + pre * (1.0 - gate)))
    ).astype(BF16)
    inner = span - 2
    total = None
    for down in range(3):
        part = None
        for right in range(3):
            piece = nt_dot(
                grad_pre[2 - right : 2 - right + inner].reshape(inner * BR, C),
                weights[3 * down + right],
            )
            part = piece if part is None else part + piece
        part = along_cycles(part.reshape(inner, BR, C + CL), down - 1)
        total = part if total is None else total + part
    table[0 : 2 * BR, :] = jnp.zeros((2 * BR, C), BF16)
    table[(WIN - 2) * BR :, :] = jnp.zeros((2 * BR, C), BF16)
    table[2 * BR : (WIN - 2) * BR, :] = total[:, :, 0:C].astype(BF16).reshape(inner * BR, C)
    order = iota((BR * BA, BR * BA), 0)
    source = iota((BR * BA, BR * BA), 1)
    swap = ((order % BA) * BR + order // BA == source).astype(F32).astype(BF16)
    own = merged[REACH - 1 : REACH - 1 + BA].reshape(BA * BR, C)
    turned = dot(swap, own)
    for cycle in range(BR):
        merged_out[cycle] = turned[BA * cycle : BA * (cycle + 1)].astype(BF16)
    own_lid = total[REACH - 2 : REACH - 2 + BA, :, C:].astype(BF16).reshape(BA * BR, CL)
    lid_out[...] = dot(swap, own_lid).astype(BF16)
    wide_table[...] = dot(spread[...], table[...]).astype(BF16)

    @pl.loop(0, ROWS // TALL_H, unroll=True)
    def _(tile):
        rows = pl.ds(pl.multiple_of(tile * TALL, TALL), TALL)
        block = feat[rows, :]
        slot_map = slots[...]
        picked = jnp.zeros((TALL_H, COLS, LANES), F32)
        for pair in range(SLOTS // 2):
            both = nt_dot(block, wide_table[pair * 2 * LANES : (pair + 1) * 2 * LANES, :])
            for side in range(2):
                value = both[:, side * LANES : (side + 1) * LANES].reshape(
                    TALL_H, COLS, LANES
                )
                picked = jnp.where((slot_map == 2 * pair + side)[None], value, picked)
        picked = picked.reshape(TALL, LANES)
        mean = jnp.sum(picked * probs[rows, :], axis=1, keepdims=True)
        grad_logits = ((picked - mean) * gain[rows, :]).astype(BF16)
        out = dot(share[rows, :], table[...]) + dot(grad_logits, depth_pad[...])
        cam_out[pl.ds(tile * TALL_H, TALL_H)] = out.astype(BF16).reshape(TALL_H, COLS, C)


def back(*operands):
    return pl.pallas_call(
        back_kernel,
        out_shape=(
            jax.ShapeDtypeStruct((BR, BA, C), BF16),
            jax.ShapeDtypeStruct((ROWS, COLS, C), BF16),
            jax.ShapeDtypeStruct((BR * BA, CL), BF16),
        ),
        in_specs=[whole(pltpu.SMEM)] + [whole()] * 14,
        out_specs=(whole(),) * 3,
        scratch_shapes=[
            pltpu.VMEM((WIN, BR, C), F32),
            pltpu.VMEM((WIN, BR, C), BF16),
            pltpu.VMEM((WIN, BR, CL), BF16),
            pltpu.VMEM((WIN * BR, C), BF16),
            pltpu.VMEM((SLOTS * LANES, C), BF16),
        ],
        compiler_params=pltpu.CompilerParams(vmem_limit_bytes=32 * 2**20),
        name="back",
    )(*operands)


def swapped(block, odd_step):
    count = lax.axis_size(AXES)
    route = [(i, (i + odd_step if i % 2 else i - odd_step) % count) for i in range(count)]
    return lax.ppermute(block, AXES, route)


def local(
    image_feats, cam_weights, depth_weight, ray_bins, pillar_sums, pillar_counts,
    lidar_weight, merge_weight, out_cotangent,
):
    me = lax.axis_index(AXES).astype(jnp.int32)
    odd = me % 2 == 1
    me = me.reshape(1)
    left_edge = image_feats[:, 0:HALO]
    right_edge = image_feats[:, COLS - HALO :]
    beside = swapped(jnp.where(odd, left_edge, right_edge), -1)
    across = swapped(jnp.where(odd, right_edge, left_edge), 1)
    pinned = lambda value: pltpu.with_memory_space_constraint(value, pltpu.HBM)
    padded, held, spread, depth_pad, masks, slots, side = prepare(
        me,
        *[
            pinned(value)
            for value in (
                image_feats, cam_weights, depth_weight.T, ray_bins, pillar_sums,
                pillar_counts.T, lidar_weight, out_cotangent,
            )
        ],
    )
    _, feat, share, lifted, note, far, probs, gain, merge_held = front(
        me, padded, across, beside, held, depth_pad, spread, masks, side,
        pinned(cam_weights), pinned(merge_weight),
    )
    partner = swapped(note, -1)
    far_got = swapped(jnp.concatenate([far, note[0:6]], 0), 3)[0:2]
    wide = lambda a: a.astype(F32)
    four = jnp.zeros((4, BR, C), F32)
    mine = lifted.reshape(WIN, BR, C)
    rise = mine[2:12] + jnp.concatenate([four, wide(partner[2:8])], 0)
    fall = mine[4:14] + jnp.concatenate([wide(partner[8:14]), four], 0)
    crossing = jnp.concatenate(
        [
            jnp.where(odd, fall, rise).astype(BF16),
            note[16:20],
            jnp.where(odd, partner[19:20], partner[16:17]),
            note[20:22],
            jnp.where(odd, partner[21:22], partner[20:21]),
        ],
        axis=0,
    )
    crossed = swapped(crossing, 1)
    relay = jnp.concatenate(
        [
            jnp.where(odd, crossed[0:6], crossed[4:10]),
            jnp.where(odd, crossed[10:11], crossed[13:14]),
            jnp.where(odd, crossed[15:16], crossed[16:17]),
        ],
        axis=0,
    )
    relayed = swapped(relay, -1)
    merged, cam_grad, lid_grad = back(
        me, lifted, note, partner, crossed, relayed, far_got, merge_held, feat, share,
        probs, gain, slots, depth_pad, spread,
    )
    return merged, cam_grad, lid_grad.reshape(BR, BA, CL)


def solution(mesh):
    columns = P(None, AXES, None)
    placed = (
        columns, P(), P(), P(AXES, None), columns, P(None, AXES), P(), P(), columns,
    )
    return jax.shard_map(
        local, mesh=mesh, in_specs=placed, out_specs=(columns,) * 3, check_vma=False
    )
```
